32 devices in a mesh: member: 2 (over y), tile: 4 (over z), day: 4 (over x, core).
Axes of the slice: x: 2, y: 2, z: 4, core: 2. Of those that a mesh axis runs over, the one named last changes fastest.
Arguments:
- fields: bfloat16 [64, 35, 16384], P(('member', 'day'), None, 'tile'), parts along dimension 0, may hold values from -6 to 6
- remap_tiles: bfloat16 [512, 128, 128], P('tile'), may hold values from 0 to 0.015625
- tile_source: int32 [512], P('tile'), may hold values from 0 to 31, as said below
- tile_band: int32 [512, 1], P('tile'), may hold values from 0 to 3, as said below
- tile_block: int32 [512], P('tile'), may hold values from 0 to 35, as said below
- patterns: bfloat16 [18432, 512], P('tile'), may hold values from -0.125 to 0.125
Outputs:
- scores: float32 [64, 35, 512], P(('member', 'day'), None, 'tile'), parts along dimension 0
The draws below stay inside these ranges and needn't reach their ends.
There are 2 independent parts, one for each index of `member`. The reference program is written for one: setup_inputs(seed, part) draws one part's arguments, and reference() takes and returns one part's arrays. A program takes and returns all parts, laid end to end along the dimension named above; an argument that names none is the same for every part. Nothing has to cross between parts.
Inputs may be any that keep to these rules, and one draw needn't show every extreme that they name: `tile_source`: index of the source block, among the 32 blocks held by the tile's own device; each of those blocks is read by some tile of that device. `tile_band`: among the 128 tiles of one device, at most 64 go to one band, and in some device exactly 64 do. `tile_block`: every target block of every band is written by at least one tile.
All inputs are finite; a program needn't handle non-finite values.
Results may differ from the reference program's by a relative error of at most 0.0039.
Values may be sent and summed in bfloat16 or wider, within the bound.
No kernel may reach another device: no remote copies, remote signals or barrier semaphores. Data moves between devices by JAX's collectives and lax.ppermute only.
A program may use at most 128 MiB of HBM per device.

```python
import jax
import jax.numpy as jnp
from jax import lax

VARS = 35
PATTERNS = 512
BLOCK = 128
SB_DEV = 32
TILES_DEV = 128
DB_DEV = 36
CAP = 64
DAYS = 32
SRC = 16384
DST = 18432
TILES = 512


def band_layout(key):
    device_count = TILES // TILES_DEV
    base = jax.random.fold_in(key, 7117)
    keys = jax.random.split(base, 5)
    devices = jnp.arange(device_count, dtype=jnp.int32)[:, None]
    block_ids = jnp.arange(DB_DEV, dtype=jnp.int32)[None, :]
    cover_band = (devices + block_ids) % device_count
    cover_block = jnp.broadcast_to(block_ids, (device_count, DB_DEV))
    band_ids = jnp.arange(device_count, dtype=jnp.int32)
    cover_count = jnp.sum((cover_band[:, :, None] == band_ids[None, None, :]).astype(jnp.int32), axis=1)
    slot_total = device_count * CAP
    slot_band = jnp.repeat(band_ids, CAP)
    slot_rank = jnp.tile(jnp.arange(CAP, dtype=jnp.int32), device_count)
    available = slot_rank[None, :] < (CAP - cover_count)[:, slot_band]
    popularity = jax.random.randint(keys[0], (device_count,), 0, 4)
    forced = jax.random.randint(keys[1], (), 0, device_count)
    noise = jax.random.randint(keys[2], (device_count, slot_total), 0, 4096)
    score = popularity[slot_band][None, :] * 4096 + noise
    boost = jnp.logical_and(devices == 0, slot_band[None, :] == forced)
    score = score + jnp.where(boost, 8 * 4096, 0)
    score = jnp.where(available, score, -1)
    score = score * slot_total + jnp.arange(slot_total, dtype=jnp.int32)[None, :]
    rest_count = TILES_DEV - DB_DEV
    _, picked = lax.top_k(score, rest_count)
    rest_band = slot_band[picked]
    rest_block = jax.random.randint(keys[3], (device_count, rest_count), 0, DB_DEV)
    bands = jnp.concatenate([cover_band, rest_band], axis=1)
    blocks = jnp.concatenate([cover_block, rest_block], axis=1)
    shuffle_keys = jax.random.randint(keys[4], (device_count, TILES_DEV), 0, 1 << 20)
    shuffle_keys = shuffle_keys * TILES_DEV + jnp.arange(TILES_DEV, dtype=jnp.int32)[None, :]
    order = jnp.argsort(shuffle_keys, axis=1)
    bands = jnp.take_along_axis(bands, order, axis=1)
    blocks = jnp.take_along_axis(blocks, order, axis=1)
    return (bands.reshape(TILES).astype(jnp.int32), blocks.reshape(TILES).astype(jnp.int32))


def draw_tile_band(key, part):
    bands, blocks = band_layout(key)
    return bands.reshape(TILES, 1)


def draw_tile_block(key, part):
    bands, blocks = band_layout(key)
    return blocks


def draw_tile_source(key, part):
    device_count = TILES // TILES_DEV
    keys = jax.random.split(jax.random.fold_in(key, 31), device_count)
    orders = jax.vmap(lambda one_key: jax.random.permutation(one_key, TILES_DEV))(keys)
    return (orders % SB_DEV).astype(jnp.int32).reshape(TILES)


def raised(entries, rng, source, target, shards_of, factor):
    owner, partner = [(jnp.arange(entries.shape[axis_at]) // (entries.shape[axis_at] // shards_of)).reshape([-1 if axis == axis_at else 1 for axis in range(entries.ndim)]) for axis_at in (source, target)]
    chosen = jax.random.permutation(rng, shards_of)[partner]
    strong = (owner == chosen) | (owner == (partner + shards_of // 2) % shards_of)
    return jnp.where(strong, factor * entries, entries)


def levels(stream_key, dims, shards, least, largest):
    factor_of = 1.0
    for position, parts in shards:
        steps = jax.random.uniform(jax.random.fold_in(jax.random.fold_in(stream_key, 6), position), (parts,), jnp.float32, least / len(shards), largest / len(shards))
        factor_of = factor_of * jnp.repeat(jnp.exp(steps), dims[position] // parts).reshape((-1,) + (1,) * (len(dims) - 1 - position))
    return factor_of


def scatter_about(key, dims, deviation, most, cuts=(), kind=jnp.bfloat16):
    entries = jax.random.normal(key, dims, jnp.float32) * deviation
    if len(cuts) > 0:
        entries = levels(key, dims, cuts, -0.22, 0.18) * entries
    return jnp.clip(entries, min=-most, max=most).astype(kind)


def noise_with(key, shape, deviation, limit, cuts, heavy, kind=jnp.bfloat16):
    values = deviation * jax.random.normal(key, shape, jnp.float32)
    if cuts:
        values = values * levels(key, shape, cuts, -0.22, 0.18)
    return jnp.clip(raised(values, jax.random.fold_in(key, 3), *heavy), -limit, limit).astype(kind)


def setup_inputs(seed: int = 0, part: int = 0) -> dict:
    streams_of = jax.random.split(jax.random.key(seed), 7)
    part_keys = jax.random.split(jax.random.fold_in(streams_of[6], part), 7)
    fields = scatter_about(part_keys[0], (DAYS, VARS, SRC), 1.0, 6.0, ((0, 4), (2, 4)))
    remap_tiles = jnp.clip(0.015625 * jax.random.uniform(streams_of[1], (TILES, BLOCK, BLOCK), jnp.float32) ** levels(streams_of[1], (TILES, BLOCK, BLOCK), ((0, 4),), -0.2, 0.2), 0.0, 0.015625).astype(jnp.bfloat16)
    tile_source = draw_tile_source(jax.random.fold_in(streams_of[6], 71), part)
    tile_band = draw_tile_band(jax.random.fold_in(streams_of[6], 71), part)
    tile_block = draw_tile_block(jax.random.fold_in(streams_of[6], 71), part)
    patterns = noise_with(streams_of[5], (DST, PATTERNS), (DB_DEV * BLOCK) ** -0.5, 0.125, ((0, 4),), (0, 1, 4, 2.0))
    return {"fields": fields, "remap_tiles": remap_tiles, "tile_source": tile_source, "tile_band": tile_band, "tile_block": tile_block, "patterns": patterns}


def reference(fields, remap_tiles, tile_source, tile_band, tile_block, patterns):
    tile_ids = jnp.arange(TILES, dtype=jnp.int32)
    source_block = (tile_ids // TILES_DEV) * SB_DEV + tile_source.astype(jnp.int32)
    target_block = tile_band[:, 0].astype(jnp.int32) * DB_DEV + tile_block.astype(jnp.int32)
    weights = remap_tiles.astype(jnp.float32)

    def one_day(day_field):
        blocked = day_field.reshape(VARS, SRC // BLOCK, BLOCK)
        columns = blocked[:, source_block, :].astype(jnp.float32)
        contrib = jnp.einsum("vtk,tkj->tvj", columns, weights).astype(jnp.bfloat16)
        summed = jax.ops.segment_sum(contrib.astype(jnp.float32), target_block, num_segments=DST // BLOCK)
        remapped = summed.astype(jnp.bfloat16).transpose(1, 0, 2).reshape(VARS, DST)
        return jnp.dot(remapped, patterns, preferred_element_type=jnp.float32)

    return lax.map(one_day, fields)
```

```python
import functools

import jax
import jax.numpy as jnp
from jax import lax
from jax.experimental import pallas as pl
from jax.experimental.pallas import tpu as pltpu
from jax.sharding import PartitionSpec as P

PLANE = ("member", "day")
VMEM_LIMIT = 56 * 2**20
LANES = 128


def pack_kernel(place, patterns, packed):
    half = packed.shape[0]
    width = LANES // 2
    offset = lax.rem(place[0], 2) * width
    lane = lax.broadcasted_iota(jnp.int32, (LANES, LANES), 1)

    @pl.loop(0, half)
    def _(j):
        first = patterns[pl.ds(pl.multiple_of(j * LANES, LANES), LANES), :]
        second = patterns[pl.ds(pl.multiple_of((j + half) * LANES, LANES), LANES), :]
        first, second = first.astype(jnp.float32), second.astype(jnp.float32)
        first = pltpu.roll(first, lax.rem(LANES - offset, LANES), 1)
        second = pltpu.roll(second, width - offset, 1)
        packed[j] = jnp.where(lane < width, first, second).astype(packed.dtype)


def pack(patterns, place):
    rows = patterns.shape[0]
    half = rows // LANES // 2
    return pl.pallas_call(
        pack_kernel,
        grid_spec=pltpu.PrefetchScalarGridSpec(
            num_scalar_prefetch=1,
            grid=(1,),
            in_specs=[pl.BlockSpec((rows, LANES), lambda i, place: (0, place[0] // 2))],
            out_specs=pl.BlockSpec((half, LANES, LANES), lambda i, place: (0, 0, 0)),
        ),
        out_shape=jax.ShapeDtypeStruct((half, LANES, LANES), patterns.dtype),
        compiler_params=pltpu.CompilerParams(vmem_limit_bytes=VMEM_LIMIT),
        name="pack",
    )(place, patterns)


def operator_kernel(slots, unroll, place, source, slot, block, weights, *rest):
    bands, packed, held, total, sems = rest[:-4], rest[-4], rest[-3], rest[-2], rest[-1]
    half = held.shape[1]
    width = LANES // 2
    copies = [
        pltpu.make_async_copy(band, held.at[pl.ds(i * slots, slots)], sems.at[i])
        for i, band in enumerate(bands)
    ]
    for copy in copies:
        copy.start()
    total[...] = jnp.zeros_like(total)
    for copy in copies:
        copy.wait()
    lane = lax.broadcasted_iota(jnp.int32, (LANES, LANES), 1)
    tiles = weights.shape[0]

    @pl.loop(0, tiles // unroll)
    def _(step):
        products = []
        for u in range(unroll):
            t = step * unroll + u
            g = block[t]
            side = g // half
            rhs = held[slot[t], g - side * half]
            keep = (lane // width) == side
            rhs = jnp.where(keep, rhs, jnp.zeros_like(rhs))
            products.append(
                jnp.dot(weights[t], rhs, preferred_element_type=jnp.float32)
            )
        for u in range(unroll):
            s = source[step * unroll + u]
            total[s] += products[u]

    blocks = total.shape[0] // 2
    swap = lax.rem(place[0], 2)

    @pl.loop(0, blocks)
    def _(j):
        first, second = total[j], total[j + blocks]
        first = first + pltpu.roll(first, width, 1)
        second = second + pltpu.roll(second, width, 1)
        packed[j] = jnp.where((lane // width) == swap, first, second).astype(packed.dtype)


def operator(weights, bands, place, source, slot, block, source_blocks, out_dtype):
    tiles = weights.shape[0]
    slots = bands[0].shape[0]
    half = bands[0].shape[1]
    scalar = pl.BlockSpec(memory_space=pltpu.SMEM)
    return pl.pallas_call(
        functools.partial(operator_kernel, slots, 4),
        in_specs=[scalar] * 4
        + [pl.BlockSpec(memory_space=pltpu.VMEM)]
        + [pl.BlockSpec(memory_space=pl.ANY)] * len(bands),
        out_specs=pl.BlockSpec(memory_space=pltpu.VMEM),
        out_shape=jax.ShapeDtypeStruct((source_blocks // 2, LANES, LANES), out_dtype),
        scratch_shapes=[
            pltpu.VMEM((slots * len(bands), half, LANES, LANES), bands[0].dtype),
            pltpu.VMEM((source_blocks, LANES, LANES), jnp.float32),
            pltpu.SemaphoreType.DMA((len(bands),)),
        ],
        compiler_params=pltpu.CompilerParams(vmem_limit_bytes=VMEM_LIMIT),
        name="operator",
    )(place, source, slot, block, weights, *bands)


def score_kernel(place, fields, *rest):
    pieces, outs = rest[:10], rest[10:]
    p, z = place[0], place[1]
    core, chip = lax.rem(p, 2), p // 2
    width = LANES // 2
    depth = fields.shape[1] // 2
    mine = pl.ds(pl.multiple_of(core * depth, depth), depth)
    other = pl.ds(pl.multiple_of((1 - core) * depth, depth), depth)
    own, far, x_own, x_far, y_own, y_far, d0_own, d0_far, d1_own, d1_far = pieces
    rows = depth // LANES
    lane = lax.broadcasted_iota(jnp.int32, (depth, LANES), 1)

    def whole(*parts):
        parts = [part[...].reshape(-1, LANES) for part in parts]
        return parts[0] if len(parts) == 1 else jnp.concatenate(parts, 0)

    sets = [
        (whole(own), whole(far)),
        (whole(x_own), whole(x_far)),
        (whole(y_own), whole(y_far)),
        (whole(d0_own, d1_own), whole(d0_far, d1_far)),
    ]
    for relative, (a, b) in enumerate(sets):
        left = jnp.where(lane < width, a, b)
        right = jnp.where(lane < width, b, a)
        r1 = jnp.dot(fields[:, mine], left, preferred_element_type=jnp.float32)
        r2 = jnp.dot(fields[:, other], right, preferred_element_type=jnp.float32)
        straight = jnp.where(core == 0, r1, r2)
        crossed = jnp.where(core == 0, r2, r1)
        value = straight + pltpu.roll(crossed, width, 1)
        chip_of = chip ^ relative
        if len(outs) == 1:
            outs[0][chip_of] = value.astype(outs[0].dtype)
        else:
            hop = lax.rem(chip_of - z + 4, 4)
            for k, out in enumerate(outs):

                @pl.when(hop == k)
                def _(out=out, value=value):
                    out[...] = value.astype(out.dtype)


def scores(fields, pieces, place, split):
    rows = fields.shape[0]
    vmem = pl.BlockSpec(memory_space=pltpu.VMEM)
    if split:
        out_shape = [jax.ShapeDtypeStruct((rows, LANES), jnp.float32)] + [
            jax.ShapeDtypeStruct((rows, LANES), jnp.bfloat16)
        ] * 3
    else:
        out_shape = [jax.ShapeDtypeStruct((4, rows, LANES), jnp.float32)]
    return pl.pallas_call(
        score_kernel,
        in_specs=[pl.BlockSpec(memory_space=pltpu.SMEM)] + [vmem] * (1 + len(pieces)),
        out_specs=[vmem] * len(out_shape),
        out_shape=out_shape,
        compiler_params=pltpu.CompilerParams(vmem_limit_bytes=VMEM_LIMIT),
        name="scores",
    )(place, fields, *pieces)


def plane_permute(x, to):
    pairs = []
    for m in range(2):
        for a in range(2):
            for c in range(2):
                tm, ta, tc = to(m, a, c)
                pairs.append((m * 4 + a * 2 + c, tm * 4 + ta * 2 + tc))
    return lax.ppermute(x, PLANE, pairs)


def over_core(x):
    return plane_permute(x, lambda m, a, c: (m, a, 1 - c))


def over_x(x):
    return plane_permute(x, lambda m, a, c: (m, 1 - a, c))


def over_y(x):
    return plane_permute(x, lambda m, a, c: (1 - m, a, c))


def on_device(fields, remap_tiles, tile_source, tile_band, tile_block, patterns):
    band_count = lax.axis_size("tile")
    day_count, var_count, source_cells = fields.shape
    row_count = day_count * var_count
    source_blocks = source_cells // LANES
    pattern_count = patterns.shape[1]
    z = lax.axis_index("tile")
    p = lax.axis_index("member") * 4 + lax.axis_index("day")
    place = jnp.stack([p, z]).astype(jnp.int32)
    owner = tile_band[:, 0]
    own = pack(patterns, place)
    if band_count == 4:
        from_left = lax.ppermute(own, "tile", [(i, (i + 1) % 4) for i in range(4)])
        from_right = lax.ppermute(own, "tile", [(i, (i + 3) % 4) for i in range(4)])
        far_right = lax.ppermute(from_right, "tile", [(1, 0), (2, 1)])
        far_left = lax.ppermute(from_left, "tile", [(1, 2), (2, 3)])
        bands = [x[None] for x in (own, from_right, far_right, far_left, from_left)]
        hop = jnp.remainder(owner - z, 4)
        slot = jnp.where(hop == 3, 4, jnp.where((hop == 2) & (z >= 2), 3, hop))
    else:
        bands = [lax.all_gather(own, "tile", axis=0)]
        slot = owner
    piece = operator(
        remap_tiles, bands, place, tile_source, slot.astype(jnp.int32), tile_block,
        source_blocks, patterns.dtype,
    )
    far = over_core(piece)
    x_own, y_own = over_x(piece), over_y(piece)
    cut = piece.shape[0] // 2
    d0_own, d1_own = over_y(x_own[:cut]), over_x(y_own[cut:])
    pieces = [piece, far]
    for part in (x_own, y_own, d0_own, d1_own):
        pieces += [part, over_core(part)]
    rows = fields.reshape(row_count, source_cells)
    parts = scores(rows, pieces, place, band_count == 4)
    if band_count == 4:
        result = parts[0]
        for k in (1, 2, 3):
            moved = lax.ppermute(parts[k], "tile", [(i, (i + k) % 4) for i in range(4)])
            result = result + moved.astype(jnp.float32)
    else:
        partial = parts[0].transpose(1, 0, 2).reshape(row_count, pattern_count)
        result = lax.psum_scatter(partial, "tile", scatter_dimension=1, tiled=True)
    return result.reshape(day_count, var_count, pattern_count // band_count)


def solution(mesh):
    return jax.shard_map(
        on_device,
        mesh=mesh,
        in_specs=(
            P(("member", "day"), None, "tile"),
            P("tile", None, None),
            P("tile"),
            P("tile", None),
            P("tile"),
            P("tile", None),
        ),
        out_specs=P(("member", "day"), None, "tile"),
        check_vma=False,
    )
```

```python
import functools

import jax
import jax.numpy as jnp
from jax import lax
from jax.experimental import pallas as pl
from jax.experimental.pallas import tpu as pltpu
from jax.sharding import PartitionSpec as P

PLANE = ("member", "day")
LANES = 128
CHUNKS = 1
GROUPS = 2 * CHUNKS
WIDTH = LANES // GROUPS
UNROLL = 16
MIB = 2**20

VMEM = pl.BlockSpec(memory_space=pltpu.VMEM)
SMEM = pl.BlockSpec(memory_space=pltpu.SMEM)
ANY = pl.BlockSpec(memory_space=pl.ANY)


def place():
    return lax.axis_index("member") * 4 + lax.axis_index("day")


def params(mib):
    return pltpu.CompilerParams(vmem_limit_bytes=mib * MIB)


def group_of(shape):
    return lax.broadcasted_iota(jnp.int32, shape, 1) // WIDTH


def pick(mask_of, values):
    out = values[-1]
    for k in range(len(values) - 2, -1, -1):
        out = jnp.where(mask_of(k), values[k], out)
    return out


def pack_kernel(parts, patterns, *rest):
    outs, held, sems = rest[:CHUNKS], rest[-2], rest[-1]
    p = place()
    chip, core = p // 2, lax.rem(p, 2)
    count = outs[0].shape[0]
    step = count // parts
    columns = pl.ds(pl.multiple_of(chip * LANES, LANES), LANES)
    copies = []
    for part in range(parts):
        for group in range(GROUPS):
            rows = pl.ds((group * count + part * step) * LANES, step * LANES)
            copies.append(
                pltpu.make_async_copy(
                    patterns.at[rows, columns], held.at[rows, :], sems.at[part, group]
                )
            )
            copies[-1].start()
    shape = (GROUPS * LANES, CHUNKS * LANES)
    k = lax.broadcasted_iota(jnp.int32, shape, 0)
    n = lax.broadcasted_iota(jnp.int32, shape, 1)
    chunk, lane_out = n // LANES, n % LANES
    wanted = chunk * (LANES // CHUNKS) + core * WIDTH + lane_out % WIDTH
    chosen = (k // LANES == lane_out // WIDTH) & (k % LANES == wanted)
    choose = jnp.where(chosen, 1.0, 0.0).astype(held.dtype)
    for part in range(parts):
        for group in range(GROUPS):
            copies[part * GROUPS + group].wait()
        for j in range(part * step, (part + 1) * step):
            blocks = [
                held[(group * count + j) * LANES : (group * count + j + 1) * LANES, :]
                for group in range(GROUPS)
            ]
            both = jnp.dot(
                jnp.concatenate(blocks, 1), choose, preferred_element_type=jnp.float32
            ).astype(held.dtype)
            for chunk in range(CHUNKS):
                outs[chunk][j] = both[:, chunk * LANES : (chunk + 1) * LANES]


def pack(patterns):
    rows = patterns.shape[0]
    count = rows // LANES // GROUPS
    parts = 3
    return pl.pallas_call(
        functools.partial(pack_kernel, parts),
        in_specs=[pl.BlockSpec(memory_space=pltpu.HBM)],
        out_specs=[VMEM] * CHUNKS,
        out_shape=[jax.ShapeDtypeStruct((count, LANES, LANES), patterns.dtype)] * CHUNKS,
        scratch_shapes=[
            pltpu.VMEM((rows, LANES), patterns.dtype),
            pltpu.SemaphoreType.DMA((parts, GROUPS)),
        ],
        compiler_params=params(8),
        name="pack",
    )(patterns)


def add_tiles(table, start, end, weights, held, total):
    group = group_of((LANES, LANES))

    @pl.loop(0, (end - start + UNROLL - 1) // UNROLL)
    def _(step):
        products, targets = [], []
        for u in range(UNROLL):
            i = start + step * UNROLL + u
            code = table[i]
            side = jnp.where(i < end, (code >> 6) & 7, 7)
            targets.append(code & 63)
            rhs = held[(code >> 9) & 1023]
            rhs = jnp.where(group == side, rhs, jnp.zeros_like(rhs))
            products.append(
                jnp.dot(weights[code >> 19], rhs, preferred_element_type=jnp.float32)
            )
        for target, product in zip(targets, products):
            total[target] += product


def early_kernel(table, weights, *rest):
    bands, total, held, sems = rest[:-3], rest[-3], rest[-2], rest[-1]
    count = bands[0].shape[0]
    copies = [
        pltpu.make_async_copy(band, held.at[pl.ds(i * count, count)], sems.at[i])
        for i, band in enumerate(bands)
    ]
    for copy in copies:
        copy.start()
    total[...] = jnp.zeros_like(total)
    for copy in copies:
        copy.wait()
    add_tiles(table, 0, table[table.shape[0] - 1], weights, held, total)


def early(table, weights, bands, source_blocks):
    count = bands[0].shape[0]
    return pl.pallas_call(
        early_kernel,
        in_specs=[SMEM, VMEM] + [ANY] * len(bands),
        out_specs=VMEM,
        out_shape=jax.ShapeDtypeStruct((source_blocks, LANES, LANES), jnp.float32),
        scratch_shapes=[
            pltpu.VMEM((count * len(bands), LANES, LANES), weights.dtype),
            pltpu.SemaphoreType.DMA((len(bands),)),
        ],
        compiler_params=params(10 + count * len(bands) * LANES * LANES * 2 // MIB),
        name="early",
    )(table, weights, *bands)


def late_kernel(table, weights, given, right, left, packed, total, held, sems):
    fetch = pltpu.make_async_copy(given, total, sems.at[0])
    fetch.start()
    first = lax.axis_index("tile") < 2

    @pl.when(first)
    def _():
        pltpu.make_async_copy(right, held, sems.at[1]).start()

    @pl.when(jnp.logical_not(first))
    def _():
        pltpu.make_async_copy(left, held, sems.at[1]).start()

    fetch.wait()
    pltpu.make_async_copy(right, held, sems.at[1]).wait()
    tiles = weights.shape[0]
    add_tiles(table, table[table.shape[0] - 1], tiles, weights, held, total)
    blocks = packed.shape[0]
    me = lax.rem(place(), GROUPS)
    group = group_of((LANES, LANES))
    for j in range(blocks):
        sums = [total[h * blocks + j] for h in range(GROUPS)]
        out = None
        for r in range(GROUPS):
            want = lax.rem(group + (r + GROUPS) - me, GROUPS)
            term = pick(lambda k: want == k, sums)
            if r:
                term = pltpu.roll(term, r * WIDTH, 1)
            out = term if out is None else out + term
        packed[j] = out.astype(packed.dtype)


def late(table, weights, total, right, left):
    source_blocks = total.shape[0]
    return pl.pallas_call(
        late_kernel,
        in_specs=[SMEM, VMEM, ANY, ANY, ANY],
        out_specs=VMEM,
        out_shape=jax.ShapeDtypeStruct((source_blocks // GROUPS, LANES, LANES), weights.dtype),
        scratch_shapes=[
            pltpu.VMEM(total.shape, jnp.float32),
            pltpu.VMEM(right.shape, weights.dtype),
            pltpu.SemaphoreType.DMA((2,)),
        ],
        compiler_params=params(14),
        name="late",
    )(table, weights, total, right, left)


def products_of(fields, pieces, flip):
    depth = fields.shape[1] // GROUPS
    across = lax.rem(place(), 4) // 2
    group = group_of((depth, LANES))
    values = [piece[...].reshape(depth, LANES) for piece in pieces]
    if CHUNKS == 1:
        sets = [[(values[0], 0), (values[1], 1)], [(values[2], 0), (values[3], 1)]]
    else:
        near, away = 2 * across, 2 * (1 - across)
        sets = [
            [(values[0], near), (values[1], near + 1), (values[2], away), (values[3], away + 1)]
        ]
    totals = [None] * len(sets)
    for h in range(GROUPS):
        rhs = []
        for members in sets:
            index = [lax.rem(i + h, GROUPS) for _, i in members]
            rhs.append(pick(lambda k: group == index[k], [value for value, _ in members]))
        rhs = jnp.concatenate(rhs, 1) if len(rhs) > 1 else rhs[0]
        product = jnp.dot(
            fields[:, h * depth : (h + 1) * depth], rhs, preferred_element_type=jnp.float32
        )
        for s in range(len(sets)):
            term = product[:, s * LANES : (s + 1) * LANES]
            if h:
                term = pltpu.roll(term, LANES - h * WIDTH, 1)
            totals[s] = term if totals[s] is None else totals[s] + term
    return totals


def by_core(even, odd, body):
    core = lax.rem(place(), 2)

    @pl.when(core == 0)
    def _():
        body(even)

    @pl.when(core == 1)
    def _():
        body(odd)


def near_kernel(fields, mine, other, r1, r2, s1, s2, out):
    def body(pieces):
        for s, total in enumerate(products_of(fields, pieces, 0)):
            out[s] = total

    by_core([mine, other, r1, r2], [other, mine, s1, s2], body)


def away_kernel(fields, r1, r2, s1, s2, d, s3, out):
    def body(pieces):
        for s, total in enumerate(products_of(fields, pieces, 1)):
            out[s] = total

    by_core([s2, s1, d, s3], [r2, r1, s3, d], body)


def last_kernel(split, fields, r1, r2, s1, s2, d, s3, *rest):
    count = 2 * CHUNKS - 1
    earlier, outs = rest[:count], rest[count:]
    p = place()
    chip = p // 2
    half = LANES // 2

    def emit(to, value):
        if not split:
            outs[0][to] = value.astype(outs[0].dtype)
            return
        hop = lax.rem(to - lax.axis_index("tile") + 4, 4)
        for k, out in enumerate(outs):

            @pl.when(hop == k)
            def _(out=out):
                out[...] = value.astype(out.dtype)

    def body(pieces):
        totals = products_of(fields, pieces, 1)
        if CHUNKS == 1:
            for relative in range(2):
                emit(chip ^ relative, earlier[0][relative])
                emit(chip ^ (2 + relative), totals[relative])
            return
        low = lax.broadcasted_iota(jnp.int32, totals[0].shape, 1) < half
        for e in range(2):
            first = earlier[e][0]
            second = totals[0] if e else earlier[2][0]
            row = 2 * ((p // 4) ^ e)
            emit(row, jnp.where(low, first, pltpu.roll(second, half, 1)))
            emit(row + 1, jnp.where(low, pltpu.roll(first, half, 1), second))

    by_core([s2, s1, d, s3], [r2, r1, s3, d], body)


def half_scores(kernel, fields, pieces, name):
    rows = fields.shape[0]
    return pl.pallas_call(
        kernel,
        in_specs=[VMEM] * (1 + len(pieces)),
        out_specs=VMEM,
        out_shape=jax.ShapeDtypeStruct((2 // CHUNKS, rows, LANES), jnp.float32),
        compiler_params=params(16),
        name=name,
    )(fields, *pieces)


def last_scores(fields, pieces, earlier, split):
    rows = fields.shape[0]
    if split:
        out_shape = [jax.ShapeDtypeStruct((rows, LANES), jnp.float32)] + [
            jax.ShapeDtypeStruct((rows, LANES), jnp.bfloat16)
        ] * 3
    else:
        out_shape = [jax.ShapeDtypeStruct((4, rows, LANES), jnp.float32)]
    return pl.pallas_call(
        functools.partial(last_kernel, split),
        in_specs=[VMEM] * (1 + len(pieces) + len(earlier)),
        out_specs=[VMEM] * len(out_shape),
        out_shape=out_shape,
        compiler_params=params(18),
        name="last",
    )(fields, *pieces, *earlier)


def plane_permute(x, to):
    pairs = []
    for m in range(2):
        for a in range(2):
            for c in range(2):
                tm, ta, tc = to(m, a, c)
                pairs.append((m * 4 + a * 2 + c, tm * 4 + ta * 2 + tc))
    return lax.ppermute(x, PLANE, pairs)


def over_core(x):
    return plane_permute(x, lambda m, a, c: (m, a, 1 - c))


def over_first(x):
    return plane_permute(x, lambda m, a, c: (m, 1 - a, c) if c == 0 else (1 - m, a, c))


def over_second(x):
    return plane_permute(x, lambda m, a, c: (1 - m, a, c) if c == 0 else (m, 1 - a, c))


def gather_plane(piece):
    other = over_core(piece)
    r1 = over_first(piece)
    r2 = over_first(other)
    d = over_second(r1)
    s1, s2, s3 = over_core(r1), over_core(r2), over_core(d)
    return (piece, other, r1, r2, s1, s2), (r1, r2, s1, s2, d, s3)


def tile_table(tile_source, tile_band, tile_block, blocks, bands, z):
    tiles = tile_source.shape[0]
    owner = tile_band[:, 0]
    if bands == 4:
        hop = jnp.remainder(owner - z, 4)
        is_late = hop == 2
        slot = jnp.where(hop == 3, 2, jnp.where(is_late, 0, hop))
    else:
        is_late = jnp.zeros_like(owner, dtype=bool)
        slot = owner
    count = blocks // GROUPS
    side = tile_block // count
    row = slot * count + tile_block - side * count
    order = jnp.arange(tiles, dtype=jnp.int32)
    code = (order << 19) | (row << 9) | (side << 6) | tile_source
    key = order + jnp.where(is_late, tiles, 0)
    rank = jnp.sum((key[None, :] < key[:, None]).astype(jnp.int32), 1)
    size = tiles + 2 * UNROLL
    place_of = jnp.arange(size, dtype=jnp.int32)
    listed = jnp.sum(jnp.where(rank[None, :] == place_of[:, None], code[None, :], 0), 1)
    soon = jnp.sum(jnp.where(is_late, 0, 1))
    return jnp.where(place_of == size - 1, soon, listed).astype(jnp.int32)


def on_device(fields, remap_tiles, tile_source, tile_band, tile_block, patterns):
    bands = lax.axis_size("tile")
    day_count, var_count, source_cells = fields.shape
    row_count = day_count * var_count
    source_blocks = source_cells // LANES
    pattern_count = patterns.shape[1]
    z = lax.axis_index("tile")
    rows = fields.transpose(1, 0, 2).reshape(row_count, source_cells)
    table = tile_table(
        tile_source, tile_band, tile_block, patterns.shape[0] // LANES, bands, z
    )
    owns = pack(patterns)
    totals, rights, lefts = [], [], []
    for own in owns:
        if bands == 4:
            from_left = lax.ppermute(own, "tile", [(i, (i + 1) % 4) for i in range(4)])
            from_right = lax.ppermute(own, "tile", [(i, (i + 3) % 4) for i in range(4)])
            rights.append(lax.ppermute(from_right, "tile", [(1, 0), (2, 1)]))
            lefts.append(lax.ppermute(from_left, "tile", [(1, 2), (2, 3)]))
            near = [own, from_right, from_left]
        else:
            gathered = lax.all_gather(own, "tile", axis=0)
            near = [gathered.reshape((-1,) + gathered.shape[2:])]
            rights.append(own)
            lefts.append(own)
        totals.append(early(table, remap_tiles, near, source_blocks))
    earlier = []
    for chunk in range(CHUNKS):
        piece = late(table, remap_tiles, totals[chunk], rights[chunk], lefts[chunk])
        near, away = gather_plane(piece)
        earlier.append(half_scores(near_kernel, rows, near, "near"))
        if chunk < CHUNKS - 1:
            earlier.append(half_scores(away_kernel, rows, away, "away"))
    parts = last_scores(rows, away, earlier, bands == 4)
    if bands == 4:
        result = parts[0]
        for k in (1, 2, 3):
            moved = lax.ppermute(parts[k], "tile", [(i, (i + k) % 4) for i in range(4)])
            result = result + moved.astype(jnp.float32)
    else:
        partial = parts[0].transpose(1, 0, 2).reshape(row_count, pattern_count)
        result = lax.psum_scatter(partial, "tile", scatter_dimension=1, tiled=True)
    return result.reshape(var_count, day_count, pattern_count // bands).transpose(1, 0, 2)


def solution(mesh):
    return jax.shard_map(
        on_device,
        mesh=mesh,
        in_specs=(
            P(("member", "day"), None, "tile"),
            P("tile", None, None),
            P("tile"),
            P("tile", None),
            P("tile"),
            P("tile", None),
        ),
        out_specs=P(("member", "day"), None, "tile"),
        check_vma=False,
    )
```

```python
import functools

import jax
import jax.numpy as jnp
from jax import lax
from jax.experimental import pallas as pl
from jax.experimental.pallas import tpu as pltpu
from jax.sharding import PartitionSpec as P

PLANE = ("member", "day")
LANES = 128
CHUNKS = 2
GROUPS = 2 * CHUNKS
WIDTH = LANES // GROUPS
UNROLL = 16
COST_EARLY = (11, 0.4)
COST_LATE = (8, 0.2)
COST_NEAR = (5, 0.6)
COST_AWAY = (5, 0.6)
DIRECT = True
TIE_EARLY = True
TIE_LATE = 0
TIE_HOP = True
TIE_SWAP = ["s1"]
TIE_RS = []
TIE_B = False
PARTS = 3
TIE_WHAT = 2
MIB = 2**20

VMEM = pl.BlockSpec(memory_space=pltpu.VMEM)
SMEM = pl.BlockSpec(memory_space=pltpu.SMEM)
ANY = pl.BlockSpec(memory_space=pl.ANY)


def place():
    return lax.axis_index("member") * 4 + lax.axis_index("day")


def params(mib):
    return pltpu.CompilerParams(vmem_limit_bytes=mib * MIB)


def cost(mib, gflop):
    return pl.CostEstimate(
        flops=int(gflop * 1e9), bytes_accessed=int(mib * MIB), transcendentals=0
    )


def group_of(shape):
    return lax.broadcasted_iota(jnp.int32, shape, 1) // WIDTH


def pick(mask_of, values):
    out = values[-1]
    for k in range(len(values) - 2, -1, -1):
        out = jnp.where(mask_of(k), values[k], out)
    return out


def pack_kernel(parts, chunk, patterns, *rest):
    out, held, sems = rest[-3:]
    p = place()
    chip, core = p // 2, lax.rem(p, 2)
    count = out.shape[0]
    step = count // parts
    columns = pl.ds(pl.multiple_of(chip * LANES, LANES), LANES)
    copies = []
    for part in range(parts):
        for group in range(GROUPS):
            rows = pl.ds((group * count + part * step) * LANES, step * LANES)
            copies.append(
                pltpu.make_async_copy(
                    patterns.at[rows, columns], held.at[rows, :], sems.at[part, group]
                )
            )
            copies[-1].start()
    shape = (GROUPS * LANES, LANES)
    k = lax.broadcasted_iota(jnp.int32, shape, 0)
    n = lax.broadcasted_iota(jnp.int32, shape, 1)
    wanted = chunk * (LANES // CHUNKS) + core * WIDTH + n % WIDTH
    chosen = (k // LANES == n // WIDTH) & (k % LANES == wanted)
    choose = jnp.where(chosen, 1.0, 0.0).astype(held.dtype)
    for part in range(parts):
        for group in range(GROUPS):
            copies[part * GROUPS + group].wait()
        for j in range(part * step, (part + 1) * step):
            blocks = [
                held[(group * count + j) * LANES : (group * count + j + 1) * LANES, :]
                for group in range(GROUPS)
            ]
            out[j] = jnp.dot(
                jnp.concatenate(blocks, 1), choose, preferred_element_type=jnp.float32
            ).astype(out.dtype)


def pack(patterns, chunk, after):
    rows = patterns.shape[0]
    count = rows // LANES // GROUPS
    parts = PARTS
    return pl.pallas_call(
        functools.partial(pack_kernel, parts, chunk),
        in_specs=[ANY] * (1 + len(after)),
        out_specs=VMEM,
        out_shape=jax.ShapeDtypeStruct((count, LANES, LANES), patterns.dtype),
        scratch_shapes=[
            pltpu.VMEM((rows, LANES), patterns.dtype),
            pltpu.SemaphoreType.DMA((parts, GROUPS)),
        ],
        compiler_params=params(58),
        cost_estimate=cost(2.3, 0.15),
        name="pack",
    )(patterns, *after)


def add_tiles(table, start, end, weights, held, total):
    group = group_of((LANES, LANES))

    @pl.loop(0, (end - start + UNROLL - 1) // UNROLL)
    def _(step):
        products, targets = [], []
        for u in range(UNROLL):
            i = start + step * UNROLL + u
            code = table[i]
            side = jnp.where(i < end, (code >> 6) & 7, 7)
            targets.append(code & 63)
            rhs = held[(code >> 9) & 1023]
            rhs = jnp.where(group == side, rhs, jnp.zeros_like(rhs))
            products.append(
                jnp.dot(weights[code >> 19], rhs, preferred_element_type=jnp.float32)
            )
        for target, product in zip(targets, products):
            total[target] += product


def early_kernel(table, weights, *rest):
    bands, total, held, sems = rest[:-3], rest[-3], rest[-2], rest[-1]
    count = bands[0].shape[0]
    copies = [
        pltpu.make_async_copy(band, held.at[pl.ds(i * count, count)], sems.at[i])
        for i, band in enumerate(bands)
    ]
    for copy in copies:
        copy.start()
    total[...] = jnp.zeros_like(total)
    for copy in copies:
        copy.wait()
    add_tiles(table, 0, table[table.shape[0] - 1], weights, held, total)


def early(table, weights, bands, source_blocks):
    count = bands[0].shape[0]
    return pl.pallas_call(
        early_kernel,
        in_specs=[SMEM, VMEM] + [ANY] * len(bands),
        out_specs=VMEM,
        out_shape=jax.ShapeDtypeStruct((source_blocks, LANES, LANES), jnp.float32),
        scratch_shapes=[
            pltpu.VMEM((count * len(bands), LANES, LANES), weights.dtype),
            pltpu.SemaphoreType.DMA((len(bands),)),
        ],
        compiler_params=params(10 + count * len(bands) * LANES * LANES * 2 // MIB),
        cost_estimate=cost(*COST_EARLY),
        name="early",
    )(table, weights, *bands)


def late_kernel(table, weights, given, right, left, packed, total, held, sems):
    fetch = pltpu.make_async_copy(given, total, sems.at[0])
    fetch.start()
    first = lax.axis_index("tile") < 2

    @pl.when(first)
    def _():
        pltpu.make_async_copy(right, held, sems.at[1]).start()

    @pl.when(jnp.logical_not(first))
    def _():
        pltpu.make_async_copy(left, held, sems.at[1]).start()

    fetch.wait()
    pltpu.make_async_copy(right, held, sems.at[1]).wait()
    tiles = weights.shape[0]
    add_tiles(table, table[table.shape[0] - 1], tiles, weights, held, total)
    blocks = packed.shape[0]
    me = lax.rem(place(), GROUPS)
    group = group_of((LANES, LANES))
    for j in range(blocks):
        sums = [total[h * blocks + j] for h in range(GROUPS)]
        out = None
        for r in range(GROUPS):
            want = lax.rem(group + (r + GROUPS) - me, GROUPS)
            term = pick(lambda k: want == k, sums)
            if r:
                term = pltpu.roll(term, r * WIDTH, 1)
            out = term if out is None else out + term
        packed[j] = out.astype(packed.dtype)


def late(table, weights, total, right, left):
    source_blocks = total.shape[0]
    return pl.pallas_call(
        late_kernel,
        in_specs=[SMEM, VMEM, ANY, ANY, ANY],
        out_specs=VMEM,
        out_shape=jax.ShapeDtypeStruct((source_blocks // GROUPS, LANES, LANES), weights.dtype),
        scratch_shapes=[
            pltpu.VMEM(total.shape, jnp.float32),
            pltpu.VMEM(right.shape, weights.dtype),
            pltpu.SemaphoreType.DMA((2,)),
        ],
        compiler_params=params(14),
        cost_estimate=cost(*COST_LATE),
        name="late",
    )(table, weights, total, right, left)


def products_of(fields, pieces):
    depth = fields.shape[1] // GROUPS
    across = lax.rem(place(), 4) // 2
    group = group_of((depth, LANES))
    values = [piece[...].reshape(depth, LANES) for piece in pieces]
    near, away = 2 * across, 2 * (1 - across)
    members = [near, near + 1, away, away + 1]
    total = None
    for h in range(GROUPS):
        index = [lax.rem(i + h, GROUPS) for i in members]
        term = jnp.dot(
            fields[:, h * depth : (h + 1) * depth],
            pick(lambda k: group == index[k], values),
            preferred_element_type=jnp.float32,
        )
        if h:
            term = pltpu.roll(term, LANES - h * WIDTH, 1)
        total = term if total is None else total + term
    return total


def by_core(even, odd, body):
    core = lax.rem(place(), 2)

    @pl.when(core == 0)
    def _():
        body(even)

    @pl.when(core == 1)
    def _():
        body(odd)


def near_kernel(fields, mine, other, *rest):
    x_even, x_odd, out = rest[:2], rest[2:4], rest[4]

    def body(pieces):
        out[...] = products_of(fields, pieces)

    by_core([mine, other, *x_even], [other, mine, *x_odd], body)


def near_scores(fields, pieces):
    rows = fields.shape[0]
    return pl.pallas_call(
        near_kernel,
        in_specs=[VMEM] * (1 + len(pieces)),
        out_specs=VMEM,
        out_shape=jax.ShapeDtypeStruct((rows, LANES), jnp.float32),
        compiler_params=params(16),
        cost_estimate=cost(*COST_NEAR),
        name="near",
    )(fields, *pieces)


def away_kernel(split, fields, *rest):
    even, odd, first, outs = rest[:4], rest[4:8], rest[8], rest[9:]
    m = place() // 4
    half = LANES // 2
    rows = fields.shape[0]
    folded = outs[0].shape[-2]

    def emit(to, value):
        if not split:
            outs[0][to] = value.astype(outs[0].dtype)
            return
        hop = lax.rem(to - lax.axis_index("tile") + 4, 4)
        for k, out in enumerate(outs):

            @pl.when(hop == k)
            def _(out=out):
                out[...] = value.astype(out.dtype)

    def body(pieces):
        low = lax.broadcasted_iota(jnp.int32, (folded, LANES), 1) < half
        for e, total in enumerate([first[...], products_of(fields, pieces)]):
            turned = pltpu.roll(total, half, 1)
            top, bottom = slice(0, folded), slice(rows - folded, rows)
            emit(2 * (m ^ e), jnp.where(low, total[top], turned[bottom]))
            emit(2 * (m ^ e) + 1, jnp.where(low, turned[top], total[bottom]))

    by_core(even, odd, body)


def away_scores(fields, pieces, near, split):
    folded = fold_rows(fields.shape[0])
    if split:
        out_shape = [jax.ShapeDtypeStruct((folded, LANES), jnp.float32)] + [
            jax.ShapeDtypeStruct((folded, LANES), jnp.bfloat16)
        ] * 3
    else:
        out_shape = [jax.ShapeDtypeStruct((4, folded, LANES), jnp.float32)]
    return pl.pallas_call(
        functools.partial(away_kernel, split),
        in_specs=[VMEM] * (2 + len(pieces)),
        out_specs=[VMEM] * len(out_shape),
        out_shape=out_shape,
        compiler_params=params(18),
        cost_estimate=cost(*COST_AWAY),
        name="away",
    )(fields, *pieces, near)


def fold_rows(rows):
    return -(-rows // 32) * 16


def final_kernel(*refs):
    parts, out = refs[:-1], refs[-1]
    rows, half = out.shape[0], LANES // 2
    folded = parts[0].shape[0]
    low = lax.broadcasted_iota(jnp.int32, (folded, LANES), 1) < half
    a, b = [
        parts[c][...] + sum(part[...].astype(jnp.float32) for part in parts[c + 1 : c + 4])
        for c in (0, 4)
    ]
    skip = 2 * folded - rows
    out[:folded, :] = jnp.where(low, a, pltpu.roll(b, half, 1))
    below = jnp.where(low, pltpu.roll(a, half, 1), b)
    out[folded:, :] = below[skip:]


def final(parts, rows):
    return pl.pallas_call(
        final_kernel,
        in_specs=[VMEM] * len(parts),
        out_specs=VMEM,
        out_shape=jax.ShapeDtypeStruct((rows, LANES), jnp.float32),
        compiler_params=params(8),
        name="final",
    )(*parts)


def plane_permute(x, to):
    pairs = []
    for m in range(2):
        for a in range(2):
            for c in range(2):
                tm, ta, tc = to(m, a, c)
                pairs.append((m * 4 + a * 2 + c, tm * 4 + ta * 2 + tc))
    return lax.ppermute(x, PLANE, pairs)


def over_core(x):
    return plane_permute(x, lambda m, a, c: (m, a, 1 - c))


def over_first(x):
    return plane_permute(x, lambda m, a, c: (m, 1 - a, c) if c == 0 else (1 - m, a, c))


def over_second(x):
    return plane_permute(x, lambda m, a, c: (1 - m, a, c) if c == 0 else (m, 1 - a, c))


def gather_plane(piece, after):
    def tie(x, name):
        return lax.optimization_barrier((x, *after[name]))[0] if after.get(name) else x

    r1 = over_first(piece)
    other = over_core(tie(piece, "other") if DIRECT else piece)
    if DIRECT:
        r2 = over_second(piece)
    else:
        r2 = over_first(other)
    d = over_second(tie(r1, "d"))
    s1, s2, s3 = over_core(tie(r1, "s1")), over_core(tie(r2, "s2")), over_core(tie(d, "s3"))
    if DIRECT:
        return (piece, other, r1, s2, s1, r2), (r2, s1, d, s3, s2, r1, s3, d), r1, r2, d
    return (piece, other, r1, r2, s1, s2), (s2, s1, d, s3, r2, r1, s3, d), r1, r2, d


def tile_table(tile_source, tile_band, tile_block, blocks, bands, z):
    tiles = tile_source.shape[0]
    owner = tile_band[:, 0]
    if bands == 4:
        hop = jnp.remainder(owner - z, 4)
        is_late = hop == 2
        slot = jnp.where(hop == 3, 2, jnp.where(is_late, 0, hop))
    else:
        is_late = jnp.zeros_like(owner, dtype=bool)
        slot = owner
    count = blocks // GROUPS
    side = tile_block // count
    row = slot * count + tile_block - side * count
    order = jnp.arange(tiles, dtype=jnp.int32)
    code = (order << 19) | (row << 9) | (side << 6) | tile_source
    key = order + jnp.where(is_late, tiles, 0)
    rank = jnp.sum((key[None, :] < key[:, None]).astype(jnp.int32), 1)
    size = tiles + 2 * UNROLL
    place_of = jnp.arange(size, dtype=jnp.int32)
    listed = jnp.sum(jnp.where(rank[None, :] == place_of[:, None], code[None, :], 0), 1)
    soon = jnp.sum(jnp.where(is_late, 0, 1))
    return jnp.where(place_of == size - 1, soon, listed).astype(jnp.int32)


def on_device(fields, remap_tiles, tile_source, tile_band, tile_block, patterns):
    bands = lax.axis_size("tile")
    day_count, var_count, source_cells = fields.shape
    row_count = day_count * var_count
    source_blocks = source_cells // LANES
    pattern_count = patterns.shape[1]
    z = lax.axis_index("tile")
    rows = fields.transpose(1, 0, 2).reshape(row_count, source_cells)
    table = tile_table(
        tile_source, tile_band, tile_block, patterns.shape[0] // LANES, bands, z
    )
    owns = []
    for chunk in range(CHUNKS):
        owns.append(pack(patterns, chunk, owns[-1:]))
    totals, rights, lefts, nears = [], [], [], []
    for own in owns:
        if bands == 4:
            from_left = lax.ppermute(own, "tile", [(i, (i + 1) % 4) for i in range(4)])
            from_right = lax.ppermute(own, "tile", [(i, (i + 3) % 4) for i in range(4)])
            near = [own, from_right, from_left]
            if totals and TIE_HOP:
                totals[-1], from_right, from_left = lax.optimization_barrier(
                    (totals[-1], from_right, from_left)
                )
            rights.append(lax.ppermute(from_right, "tile", [(1, 0), (2, 1)]))
            lefts.append(lax.ppermute(from_left, "tile", [(1, 2), (2, 3)]))
        else:
            gathered = lax.all_gather(own, "tile", axis=0)
            near = [gathered.reshape((-1,) + gathered.shape[2:])]
            rights.append(own)
            lefts.append(own)
        nears.append(near)
        if TIE_B and len(nears) == 2:
            continue
        totals.append(early(table, remap_tiles, near, source_blocks))
    if TIE_EARLY and not TIE_B:
        totals = list(lax.optimization_barrier(totals))
    sums, done = [], {}
    for chunk in range(CHUNKS):
        piece = late(table, remap_tiles, totals[chunk], rights[chunk], lefts[chunk])
        if TIE_B and chunk == 0:
            own, *_ = lax.optimization_barrier((nears[1][0], piece))
            totals.append(early(table, remap_tiles, [own, *nears[1][1:]], source_blocks))
        near, away, r1, r2, d = gather_plane(piece, done)
        if chunk == 0 and TIE_LATE:
            tied = {1: near[1:2], 2: (r1,), 3: (r2,), 4: (d,), 5: (r1, near[1])}[TIE_LATE]
            totals[1], *_ = lax.optimization_barrier((totals[1], *tied))
        if done_near := done.get("near"):
            near = lax.optimization_barrier((*near, *done_near))[: len(near)]
        part = near_scores(rows, near)
        parts = list(away_scores(rows, away, part, bands == 4))
        done = {}
        for name in TIE_SWAP:
            done.setdefault(name, []).append(part if TIE_WHAT == 1 else parts[0])
        if bands == 4:
            for k in (1, 2, 3):
                pairs = [(i, (i + k) % 4) for i in range(4)]
                parts[k] = lax.ppermute(parts[k], "tile", pairs)
            sums += parts
            for name in TIE_RS:
                done.setdefault(name, []).extend(parts[1:4])
        else:
            folded = parts[0]
            half, skip = LANES // 2, 2 * folded.shape[1] - row_count
            sums.append(
                jnp.concatenate([folded[:, :, :half], folded[:, skip:, half:]], 1)
            )
    if bands == 4:
        result = final(sums, row_count)
    else:
        partial = jnp.concatenate(sums, 2).transpose(1, 0, 2).reshape(row_count, pattern_count)
        result = lax.psum_scatter(partial, "tile", scatter_dimension=1, tiled=True)
    return result.reshape(var_count, day_count, pattern_count // bands).transpose(1, 0, 2)


def solution(mesh):
    return jax.shard_map(
        on_device,
        mesh=mesh,
        in_specs=(
            P(("member", "day"), None, "tile"),
            P("tile", None, None),
            P("tile"),
            P("tile", None),
            P("tile"),
            P("tile", None),
        ),
        out_specs=P(("member", "day"), None, "tile"),
        check_vma=False,
    )
```

```python
import functools

import jax
import jax.numpy as jnp
from jax import lax
from jax.experimental import pallas as pl
from jax.experimental.pallas import tpu as pltpu
from jax.sharding import PartitionSpec as P

PLANE = ("member", "day")
LANES = 128
CHUNKS = 2
GROUPS = 2 * CHUNKS
WIDTH = LANES // GROUPS
UNROLL = 16
COST_EARLY = (11, 0.4)
COST_LATE = (8, 0.2)
COST_NEAR = [(5, 0.6), (5, 0.6)]
COST_AWAY = [(5, 0.6), (5, 0.6)]
DIRECT = True
MERGED = True
TIE_LATE = []
TIE_SWAP = {'s1': ['near'], 's2': ['near']}
TIE_NEAR = []
PARTS = 3
MIB = 2**20

VMEM = pl.BlockSpec(memory_space=pltpu.VMEM)
SMEM = pl.BlockSpec(memory_space=pltpu.SMEM)
ANY = pl.BlockSpec(memory_space=pl.ANY)


def place():
    return lax.axis_index("member") * 4 + lax.axis_index("day")


def params(mib):
    return pltpu.CompilerParams(vmem_limit_bytes=mib * MIB)


def cost(mib, gflop):
    return pl.CostEstimate(
        flops=int(gflop * 1e9), bytes_accessed=int(mib * MIB), transcendentals=0
    )


def group_of(shape):
    return lax.broadcasted_iota(jnp.int32, shape, 1) // WIDTH


def pick(mask_of, values):
    out = values[-1]
    for k in range(len(values) - 2, -1, -1):
        out = jnp.where(mask_of(k), values[k], out)
    return out


def pack_kernel(parts, chunk, patterns, *rest):
    out, held, sems = rest[-3:]
    p = place()
    chip, core = p // 2, lax.rem(p, 2)
    count = out.shape[0]
    step = count // parts
    columns = pl.ds(pl.multiple_of(chip * LANES, LANES), LANES)
    copies = []
    for part in range(parts):
        for group in range(GROUPS):
            rows = pl.ds((group * count + part * step) * LANES, step * LANES)
            copies.append(
                pltpu.make_async_copy(
                    patterns.at[rows, columns], held.at[rows, :], sems.at[part, group]
                )
            )
            copies[-1].start()
    shape = (GROUPS * LANES, LANES)
    k = lax.broadcasted_iota(jnp.int32, shape, 0)
    n = lax.broadcasted_iota(jnp.int32, shape, 1)
    wanted = chunk * (LANES // CHUNKS) + core * WIDTH + n % WIDTH
    chosen = (k // LANES == n // WIDTH) & (k % LANES == wanted)
    choose = jnp.where(chosen, 1.0, 0.0).astype(held.dtype)
    for part in range(parts):
        for group in range(GROUPS):
            copies[part * GROUPS + group].wait()
        for j in range(part * step, (part + 1) * step):
            blocks = [
                held[(group * count + j) * LANES : (group * count + j + 1) * LANES, :]
                for group in range(GROUPS)
            ]
            out[j] = jnp.dot(
                jnp.concatenate(blocks, 1), choose, preferred_element_type=jnp.float32
            ).astype(out.dtype)


def pack(patterns, chunk, after):
    rows = patterns.shape[0]
    count = rows // LANES // GROUPS
    parts = PARTS
    return pl.pallas_call(
        functools.partial(pack_kernel, parts, chunk),
        in_specs=[ANY] * (1 + len(after)),
        out_specs=VMEM,
        out_shape=jax.ShapeDtypeStruct((count, LANES, LANES), patterns.dtype),
        scratch_shapes=[
            pltpu.VMEM((rows, LANES), patterns.dtype),
            pltpu.SemaphoreType.DMA((parts, GROUPS)),
        ],
        compiler_params=params(58),
        cost_estimate=cost(2.3, 0.15),
        name="pack",
    )(patterns, *after)


def add_tiles(table, start, end, weights, held, total):
    group = group_of((LANES, LANES))

    @pl.loop(0, (end - start + UNROLL - 1) // UNROLL)
    def _(step):
        products, targets = [], []
        for u in range(UNROLL):
            i = start + step * UNROLL + u
            code = table[i]
            side = jnp.where(i < end, (code >> 6) & 7, 7)
            targets.append(code & 63)
            rhs = held[(code >> 9) & 1023]
            rhs = jnp.where(group == side, rhs, jnp.zeros_like(rhs))
            products.append(
                jnp.dot(weights[code >> 19], rhs, preferred_element_type=jnp.float32)
            )
        for target, product in zip(targets, products):
            total[target] += product


def early_kernel(table, weights, *rest):
    bands, total, held, sems = rest[:-3], rest[-3], rest[-2], rest[-1]
    count = bands[0].shape[0]
    copies = [
        pltpu.make_async_copy(band, held.at[pl.ds(i * count, count)], sems.at[i])
        for i, band in enumerate(bands)
    ]
    for copy in copies:
        copy.start()
    total[...] = jnp.zeros_like(total)
    for copy in copies:
        copy.wait()
    add_tiles(table, 0, table[table.shape[0] - 1], weights, held, total)


def early(table, weights, bands, source_blocks):
    count = bands[0].shape[0]
    return pl.pallas_call(
        early_kernel,
        in_specs=[SMEM, VMEM] + [ANY] * len(bands),
        out_specs=VMEM,
        out_shape=jax.ShapeDtypeStruct((source_blocks, LANES, LANES), jnp.float32),
        scratch_shapes=[
            pltpu.VMEM((count * len(bands), LANES, LANES), weights.dtype),
            pltpu.SemaphoreType.DMA((len(bands),)),
        ],
        compiler_params=params(10 + count * len(bands) * LANES * LANES * 2 // MIB),
        cost_estimate=cost(*COST_EARLY),
        name="early",
    )(table, weights, *bands)


def late_kernel(table, weights, given, right, left, packed, total, held, sems):
    fetch = pltpu.make_async_copy(given, total, sems.at[0])
    fetch.start()
    first = lax.axis_index("tile") < 2

    @pl.when(first)
    def _():
        pltpu.make_async_copy(right, held, sems.at[1]).start()

    @pl.when(jnp.logical_not(first))
    def _():
        pltpu.make_async_copy(left, held, sems.at[1]).start()

    fetch.wait()
    pltpu.make_async_copy(right, held, sems.at[1]).wait()
    tiles = weights.shape[0]
    add_tiles(table, table[table.shape[0] - 1], tiles, weights, held, total)
    blocks = packed.shape[0]
    me = lax.rem(place(), GROUPS)
    group = group_of((LANES, LANES))
    for j in range(blocks):
        sums = [total[h * blocks + j] for h in range(GROUPS)]
        out = None
        for r in range(GROUPS):
            want = lax.rem(group + (r + GROUPS) - me, GROUPS)
            term = pick(lambda k: want == k, sums)
            if r:
                term = pltpu.roll(term, r * WIDTH, 1)
            out = term if out is None else out + term
        packed[j] = out.astype(packed.dtype)


def late(table, weights, total, right, left):
    source_blocks = total.shape[0]
    return pl.pallas_call(
        late_kernel,
        in_specs=[SMEM, VMEM, ANY, ANY, ANY],
        out_specs=VMEM,
        out_shape=jax.ShapeDtypeStruct((source_blocks // GROUPS, LANES, LANES), weights.dtype),
        scratch_shapes=[
            pltpu.VMEM(total.shape, jnp.float32),
            pltpu.VMEM(right.shape, weights.dtype),
            pltpu.SemaphoreType.DMA((2,)),
        ],
        compiler_params=params(14),
        cost_estimate=cost(*COST_LATE),
        name="late",
    )(table, weights, total, right, left)


def products_of(fields, pieces):
    depth = fields.shape[1] // GROUPS
    across = lax.rem(place(), 4) // 2
    group = group_of((depth, LANES))
    values = [piece[...].reshape(depth, LANES) for piece in pieces]
    near, away = 2 * across, 2 * (1 - across)
    members = [near, near + 1, away, away + 1]
    total = None
    for h in range(GROUPS):
        index = [lax.rem(i + h, GROUPS) for i in members]
        term = jnp.dot(
            fields[:, h * depth : (h + 1) * depth],
            pick(lambda k: group == index[k], values),
            preferred_element_type=jnp.float32,
        )
        if h:
            term = pltpu.roll(term, LANES - h * WIDTH, 1)
        total = term if total is None else total + term
    return total


def by_core(even, odd, body):
    core = lax.rem(place(), 2)

    @pl.when(core == 0)
    def _():
        body(even)

    @pl.when(core == 1)
    def _():
        body(odd)


def near_kernel(fields, mine, other, *rest):
    x_even, x_odd, out = rest[:2], rest[2:4], rest[4]

    def body(pieces):
        out[...] = products_of(fields, pieces)

    by_core([mine, other, *x_even], [other, mine, *x_odd], body)


def near_scores(fields, pieces, chunk):
    rows = fields.shape[0]
    return pl.pallas_call(
        near_kernel,
        in_specs=[VMEM] * (1 + len(pieces)),
        out_specs=VMEM,
        out_shape=jax.ShapeDtypeStruct((rows, LANES), jnp.float32),
        compiler_params=params(16),
        cost_estimate=cost(*COST_NEAR[chunk]),
        name="near",
    )(fields, *pieces)


def away_kernel(split, fields, *rest):
    even, odd, first, outs = rest[:4], rest[4:8], rest[8], rest[9:]
    m = place() // 4
    half = LANES // 2
    rows = fields.shape[0]
    folded = outs[0].shape[-2]

    def emit(to, value):
        if not split:
            outs[0][to] = value.astype(outs[0].dtype)
            return
        hop = lax.rem(to - lax.axis_index("tile") + 4, 4)
        for k, out in enumerate(outs):

            @pl.when(hop == k)
            def _(out=out):
                out[...] = value.astype(out.dtype)

    def body(pieces):
        low = lax.broadcasted_iota(jnp.int32, (folded, LANES), 1) < half
        for e, total in enumerate([first[...], products_of(fields, pieces)]):
            turned = pltpu.roll(total, half, 1)
            top, bottom = slice(0, folded), slice(rows - folded, rows)
            emit(2 * (m ^ e), jnp.where(low, total[top], turned[bottom]))
            emit(2 * (m ^ e) + 1, jnp.where(low, turned[top], total[bottom]))

    by_core(even, odd, body)


def away_scores(fields, pieces, near, split, chunk):
    folded = fold_rows(fields.shape[0])
    if split:
        out_shape = [jax.ShapeDtypeStruct((folded, LANES), jnp.float32)] + [
            jax.ShapeDtypeStruct((folded, LANES), jnp.bfloat16)
        ] * 3
    else:
        out_shape = [jax.ShapeDtypeStruct((4, folded, LANES), jnp.float32)]
    return pl.pallas_call(
        functools.partial(away_kernel, split),
        in_specs=[VMEM] * (2 + len(pieces)),
        out_specs=[VMEM] * len(out_shape),
        out_shape=out_shape,
        compiler_params=params(18),
        cost_estimate=cost(*COST_AWAY[chunk]),
        name="away",
    )(fields, *pieces, near)


def raw_kernel(fields, *rest):
    even, odd, out = rest[:4], rest[4:8], rest[8]

    def body(pieces):
        out[...] = products_of(fields, pieces)

    by_core(even, odd, body)


def raw_scores(fields, pieces, chunk):
    rows = fields.shape[0]
    return pl.pallas_call(
        raw_kernel,
        in_specs=[VMEM] * (1 + len(pieces)),
        out_specs=VMEM,
        out_shape=jax.ShapeDtypeStruct((rows, LANES), jnp.float32),
        compiler_params=params(16),
        cost_estimate=cost(*COST_AWAY[chunk]),
        name="raw",
    )(fields, *pieces)


def last_kernel(split, fields, *rest):
    even, odd, earlier, outs = rest[:4], rest[4:8], rest[8:11], rest[11:]
    m = place() // 4
    half = LANES // 2
    low = lax.broadcasted_iota(jnp.int32, earlier[0].shape, 1) < half

    def emit(to, value):
        if not split:
            outs[0][to] = value.astype(outs[0].dtype)
            return
        hop = lax.rem(to - lax.axis_index("tile") + 4, 4)
        for k, out in enumerate(outs):

            @pl.when(hop == k)
            def _(out=out):
                out[...] = value.astype(out.dtype)

    def body(pieces):
        second = products_of(fields, pieces)
        pairs = [(earlier[0][...], earlier[2][...]), (earlier[1][...], second)]
        for e, (a, b) in enumerate(pairs):
            emit(2 * (m ^ e), jnp.where(low, a, pltpu.roll(b, half, 1)))
            emit(2 * (m ^ e) + 1, jnp.where(low, pltpu.roll(a, half, 1), b))

    by_core(even, odd, body)


def last_scores(fields, pieces, earlier, split):
    rows = fields.shape[0]
    if split:
        out_shape = [jax.ShapeDtypeStruct((rows, LANES), jnp.float32)] + [
            jax.ShapeDtypeStruct((rows, LANES), jnp.bfloat16)
        ] * 3
    else:
        out_shape = [jax.ShapeDtypeStruct((4, rows, LANES), jnp.float32)]
    return pl.pallas_call(
        functools.partial(last_kernel, split),
        in_specs=[VMEM] * (1 + len(pieces) + len(earlier)),
        out_specs=[VMEM] * len(out_shape),
        out_shape=out_shape,
        compiler_params=params(18),
        cost_estimate=cost(*COST_AWAY[1]),
        name="last",
    )(fields, *pieces, *earlier)


def fold_rows(rows):
    return -(-rows // 32) * 16


def final_kernel(*refs):
    parts, out = refs[:-1], refs[-1]
    rows, half = out.shape[0], LANES // 2
    folded = parts[0].shape[0]
    low = lax.broadcasted_iota(jnp.int32, (folded, LANES), 1) < half
    a, b = [
        parts[c][...] + sum(part[...].astype(jnp.float32) for part in parts[c + 1 : c + 4])
        for c in (0, 4)
    ]
    skip = 2 * folded - rows
    out[:folded, :] = jnp.where(low, a, pltpu.roll(b, half, 1))
    below = jnp.where(low, pltpu.roll(a, half, 1), b)
    out[folded:, :] = below[skip:]


def final(parts, rows):
    return pl.pallas_call(
        final_kernel,
        in_specs=[VMEM] * len(parts),
        out_specs=VMEM,
        out_shape=jax.ShapeDtypeStruct((rows, LANES), jnp.float32),
        compiler_params=params(8),
        name="final",
    )(*parts)


def plane_permute(x, to):
    pairs = []
    for m in range(2):
        for a in range(2):
            for c in range(2):
                tm, ta, tc = to(m, a, c)
                pairs.append((m * 4 + a * 2 + c, tm * 4 + ta * 2 + tc))
    return lax.ppermute(x, PLANE, pairs)


def over_core(x):
    return plane_permute(x, lambda m, a, c: (m, a, 1 - c))


def over_first(x):
    return plane_permute(x, lambda m, a, c: (m, 1 - a, c) if c == 0 else (1 - m, a, c))


def over_second(x):
    return plane_permute(x, lambda m, a, c: (1 - m, a, c) if c == 0 else (m, 1 - a, c))


def gather_plane(piece, after):
    def tie(x, name):
        return lax.optimization_barrier((x, *after[name]))[0] if after.get(name) else x

    r1 = over_first(piece)
    other = over_core(tie(piece, "other") if DIRECT else piece)
    if DIRECT:
        r2 = over_second(tie(piece, "r2"))
    else:
        r2 = over_first(tie(other, "r2"))
    d = over_second(tie(r1, "d"))
    s1, s2, s3 = over_core(tie(r1, "s1")), over_core(tie(r2, "s2")), over_core(tie(d, "s3"))
    if DIRECT:
        return (piece, other, r1, s2, s1, r2), (r2, s1, d, s3, s2, r1, s3, d), r1, r2, d
    return (piece, other, r1, r2, s1, s2), (s2, s1, d, s3, r2, r1, s3, d), r1, r2, d


def tile_table(tile_source, tile_band, tile_block, blocks, bands, z):
    tiles = tile_source.shape[0]
    owner = tile_band[:, 0]
    if bands == 4:
        hop = jnp.remainder(owner - z, 4)
        is_late = hop == 2
        slot = jnp.where(hop == 3, 2, jnp.where(is_late, 0, hop))
    else:
        is_late = jnp.zeros_like(owner, dtype=bool)
        slot = owner
    count = blocks // GROUPS
    side = tile_block // count
    row = slot * count + tile_block - side * count
    order = jnp.arange(tiles, dtype=jnp.int32)
    code = (order << 19) | (row << 9) | (side << 6) | tile_source
    key = order + jnp.where(is_late, tiles, 0)
    rank = jnp.sum((key[None, :] < key[:, None]).astype(jnp.int32), 1)
    size = tiles + 2 * UNROLL
    place_of = jnp.arange(size, dtype=jnp.int32)
    listed = jnp.sum(jnp.where(rank[None, :] == place_of[:, None], code[None, :], 0), 1)
    soon = jnp.sum(jnp.where(is_late, 0, 1))
    return jnp.where(place_of == size - 1, soon, listed).astype(jnp.int32)


def on_device(fields, remap_tiles, tile_source, tile_band, tile_block, patterns):
    bands = lax.axis_size("tile")
    day_count, var_count, source_cells = fields.shape
    row_count = day_count * var_count
    source_blocks = source_cells // LANES
    pattern_count = patterns.shape[1]
    z = lax.axis_index("tile")
    rows = fields.transpose(1, 0, 2).reshape(row_count, source_cells)
    table = tile_table(
        tile_source, tile_band, tile_block, patterns.shape[0] // LANES, bands, z
    )
    owns, totals, rights, lefts = [], [], [], []
    for chunk in range(CHUNKS):
        own = pack(patterns, chunk, owns[-1:])
        owns.append(own)
        if bands == 4:
            from_left = lax.ppermute(own, "tile", [(i, (i + 1) % 4) for i in range(4)])
            from_right = lax.ppermute(own, "tile", [(i, (i + 3) % 4) for i in range(4)])
            near = [own, from_right, from_left]
            if chunk:
                totals[-1], from_right, from_left = lax.optimization_barrier(
                    (totals[-1], from_right, from_left)
                )
            rights.append(lax.ppermute(from_right, "tile", [(1, 0), (2, 1)]))
            lefts.append(lax.ppermute(from_left, "tile", [(1, 2), (2, 3)]))
        else:
            gathered = lax.all_gather(own, "tile", axis=0)
            near = [gathered.reshape((-1,) + gathered.shape[2:])]
            rights.append(own)
            lefts.append(own)
        totals.append(early(table, remap_tiles, near, source_blocks))
    totals = list(lax.optimization_barrier(totals))
    sums, past, raw = [], {}, []
    for chunk in range(CHUNKS):

        def after(x, names):
            held = [past[name] for name in names if name in past]
            return lax.optimization_barrier((x, *held))[0] if held else x

        total = after(totals[chunk], TIE_LATE)
        piece = late(table, remap_tiles, total, rights[chunk], lefts[chunk])
        near, away, r1, r2, d = gather_plane(piece, {k: [past[n] for n in v if n in past] for k, v in TIE_SWAP.items()})
        part = near_scores(rows, [after(near[0], TIE_NEAR), *near[1:]], chunk)
        raw.append(part)
        if MERGED and chunk == 0:
            far_part = raw_scores(rows, away, chunk)
            raw.append(far_part)
            past = dict(piece=piece, other=near[1], r1=r1, r2=r2, d=d, near=part, away=far_part)
            continue
        if MERGED:
            parts = list(last_scores(rows, away, raw, bands == 4))
        else:
            parts = list(away_scores(rows, away, part, bands == 4, chunk))
        past = dict(piece=piece, other=near[1], r1=r1, r2=r2, d=d, near=part, away=parts[0])
        if bands == 4:
            for k in (1, 2, 3):
                pairs = [(i, (i + k) % 4) for i in range(4)]
                parts[k] = lax.ppermute(parts[k], "tile", pairs)
            sums += parts
            past["sum1"], past["sum2"], past["sum3"] = parts[1:]
        elif MERGED:
            sums.append(parts[0])
        else:
            folded = parts[0]
            half, skip = LANES // 2, 2 * folded.shape[1] - row_count
            sums.append(
                jnp.concatenate([folded[:, :, :half], folded[:, skip:, half:]], 1)
            )
    if bands == 4:
        if MERGED:
            result = sums[0]
            for moved in sums[1:]:
                result = result + moved.astype(jnp.float32)
        else:
            result = final(sums, row_count)
    else:
        partial = jnp.concatenate(sums, 2).transpose(1, 0, 2).reshape(row_count, pattern_count)
        result = lax.psum_scatter(partial, "tile", scatter_dimension=1, tiled=True)
    return result.reshape(var_count, day_count, pattern_count // bands).transpose(1, 0, 2)


def solution(mesh):
    return jax.shard_map(
        on_device,
        mesh=mesh,
        in_specs=(
            P(("member", "day"), None, "tile"),
            P("tile", None, None),
            P("tile"),
            P("tile", None),
            P("tile"),
            P("tile", None),
        ),
        out_specs=P(("member", "day"), None, "tile"),
        check_vma=False,
    )
```

```python
import functools

import jax
import jax.numpy as jnp
from jax import lax
from jax.experimental import pallas as pl
from jax.experimental.pallas import tpu as pltpu
from jax.sharding import PartitionSpec as P

PLANE = ("member", "day")
LANES = 128
CHUNKS = 2
GROUPS = 2 * CHUNKS
WIDTH = LANES // GROUPS
UNROLL = 32
EARLY = 32
LATE = 16
COST_EARLY = (11, 0.4)
COST_LATE = (8, 0.2)
COST_NEAR = [(5, 0.6), (5, 0.6)]
COST_AWAY = [(5, 0.6), (5, 0.6)]
DIRECT = True
MERGED = True
TIE_LATE = []
TIE_OWN = True
TIE_HOP = True
TIE_EARLY = False
TIE_SWAP = {'s1': ['near'], 's2': ['near']}
TIE_NEAR = []
PARTS = 1
MIB = 2**20

VMEM = pl.BlockSpec(memory_space=pltpu.VMEM)
SMEM = pl.BlockSpec(memory_space=pltpu.SMEM)
ANY = pl.BlockSpec(memory_space=pl.ANY)


def place():
    return lax.axis_index("member") * 4 + lax.axis_index("day")


def params(mib):
    return pltpu.CompilerParams(vmem_limit_bytes=mib * MIB)


def cost(mib, gflop):
    return pl.CostEstimate(
        flops=int(gflop * 1e9), bytes_accessed=int(mib * MIB), transcendentals=0
    )


def group_of(shape):
    return lax.broadcasted_iota(jnp.int32, shape, 1) // WIDTH


def pick(mask_of, values):
    out = values[-1]
    for k in range(len(values) - 2, -1, -1):
        out = jnp.where(mask_of(k), values[k], out)
    return out


def pack_kernel(parts, chunk, patterns, *rest):
    out, held, sems = rest[-3:]
    p = place()
    chip, core = p // 2, lax.rem(p, 2)
    count = out.shape[0]
    step = count // parts
    columns = pl.ds(pl.multiple_of(chip * LANES, LANES), LANES)
    copies = []
    for part in range(parts):
        for group in range(GROUPS):
            rows = pl.ds((group * count + part * step) * LANES, step * LANES)
            copies.append(
                pltpu.make_async_copy(
                    patterns.at[rows, columns], held.at[rows, :], sems.at[part, group]
                )
            )
            copies[-1].start()
    shape = (GROUPS * LANES, LANES)
    k = lax.broadcasted_iota(jnp.int32, shape, 0)
    n = lax.broadcasted_iota(jnp.int32, shape, 1)
    wanted = chunk * (LANES // CHUNKS) + core * WIDTH + n % WIDTH
    chosen = (k // LANES == n // WIDTH) & (k % LANES == wanted)
    choose = jnp.where(chosen, 1.0, 0.0).astype(held.dtype)
    for part in range(parts):
        for group in range(GROUPS):
            copies[part * GROUPS + group].wait()
        blocks = [
            held[pl.ds((group * count + part * step) * LANES, step * LANES), :]
            for group in range(GROUPS)
        ]
        both = jnp.dot(jnp.concatenate(blocks, 1), choose, preferred_element_type=jnp.float32)
        out[part * step : (part + 1) * step] = both.astype(out.dtype).reshape(step, LANES, LANES)


def pack(patterns, chunk, after):
    rows = patterns.shape[0]
    count = rows // LANES // GROUPS
    parts = PARTS
    return pl.pallas_call(
        functools.partial(pack_kernel, parts, chunk),
        in_specs=[ANY] * (1 + len(after)),
        out_specs=VMEM,
        out_shape=jax.ShapeDtypeStruct((count, LANES, LANES), patterns.dtype),
        scratch_shapes=[
            pltpu.VMEM((rows, LANES), patterns.dtype),
            pltpu.SemaphoreType.DMA((parts, GROUPS)),
        ],
        compiler_params=params(58),
        cost_estimate=cost(2.3, 0.15),
        name="pack",
    )(patterns, *after)


def add_tiles(unroll, table, start, end, weights, held, total):
    group = group_of((LANES, LANES))

    @pl.loop(0, (end - start + unroll - 1) // unroll)
    def _(step):
        products, targets = [], []
        for u in range(unroll):
            i = start + step * unroll + u
            code = table[i]
            side = jnp.where(i < end, (code >> 6) & 7, 7)
            targets.append(code & 63)
            rhs = held[(code >> 9) & 1023]
            rhs = jnp.where(group == side, rhs, jnp.zeros_like(rhs))
            products.append(
                jnp.dot(weights[code >> 19], rhs, preferred_element_type=jnp.float32)
            )
        for target, product in zip(targets, products):
            total[target] += product


def early_kernel(table, weights, *rest):
    bands, total, held, sems = rest[:-3], rest[-3], rest[-2], rest[-1]
    count = bands[0].shape[0]
    copies = [
        pltpu.make_async_copy(band, held.at[pl.ds(i * count, count)], sems.at[i])
        for i, band in enumerate(bands)
    ]
    for copy in copies:
        copy.start()
    total[...] = jnp.zeros_like(total)
    for copy in copies:
        copy.wait()
    add_tiles(EARLY, table, 0, table[table.shape[0] - 1], weights, held, total)


def early(table, weights, bands, source_blocks):
    count = bands[0].shape[0]
    return pl.pallas_call(
        early_kernel,
        in_specs=[SMEM, VMEM] + [ANY] * len(bands),
        out_specs=VMEM,
        out_shape=jax.ShapeDtypeStruct((source_blocks, LANES, LANES), jnp.float32),
        scratch_shapes=[
            pltpu.VMEM((count * len(bands), LANES, LANES), weights.dtype),
            pltpu.SemaphoreType.DMA((len(bands),)),
        ],
        compiler_params=params(10 + count * len(bands) * LANES * LANES * 2 // MIB),
        cost_estimate=cost(*COST_EARLY),
        name="early",
    )(table, weights, *bands)


def late_kernel(table, weights, given, band, packed, total):
    total[...] = jnp.zeros_like(total)
    start = table[table.shape[0] - 1]
    add_tiles(LATE, table, start, weights.shape[0], weights, band, total)
    blocks = packed.shape[0]
    me = lax.rem(place(), GROUPS)
    group = group_of((LANES, LANES))
    for j in range(blocks):
        places = [h * blocks + j for h in range(GROUPS)]
        sums = [given[i] + total[i] for i in places]
        out = None
        for r in range(GROUPS):
            want = lax.rem(group + (r + GROUPS) - me, GROUPS)
            term = pick(lambda k: want == k, sums)
            if r:
                term = pltpu.roll(term, r * WIDTH, 1)
            out = term if out is None else out + term
        packed[j] = out.astype(packed.dtype)


def late(table, weights, total, band):
    source_blocks = total.shape[0]
    return pl.pallas_call(
        late_kernel,
        in_specs=[SMEM, VMEM, VMEM, VMEM],
        out_specs=VMEM,
        out_shape=jax.ShapeDtypeStruct((source_blocks // GROUPS, LANES, LANES), weights.dtype),
        scratch_shapes=[
            pltpu.VMEM(total.shape, jnp.float32),
        ],
        compiler_params=params(14),
        cost_estimate=cost(*COST_LATE),
        name="late",
    )(table, weights, total, band)


def products_of(fields, pieces):
    depth = fields.shape[1] // GROUPS
    across = lax.rem(place(), 4) // 2
    group = group_of((depth, LANES))
    values = [piece[...].reshape(depth, LANES) for piece in pieces]
    near, away = 2 * across, 2 * (1 - across)
    members = [near, near + 1, away, away + 1]
    total = None
    for h in range(GROUPS):
        index = [lax.rem(i + h, GROUPS) for i in members]
        term = jnp.dot(
            fields[:, h * depth : (h + 1) * depth],
            pick(lambda k: group == index[k], values),
            preferred_element_type=jnp.float32,
        )
        if h:
            term = pltpu.roll(term, LANES - h * WIDTH, 1)
        total = term if total is None else total + term
    return total


def by_core(even, odd, body):
    core = lax.rem(place(), 2)

    @pl.when(core == 0)
    def _():
        body(even)

    @pl.when(core == 1)
    def _():
        body(odd)


def near_kernel(fields, mine, other, *rest):
    x_even, x_odd, out = rest[:2], rest[2:4], rest[4]

    def body(pieces):
        out[...] = products_of(fields, pieces)

    by_core([mine, other, *x_even], [other, mine, *x_odd], body)


def near_scores(fields, pieces, chunk):
    rows = fields.shape[0]
    return pl.pallas_call(
        near_kernel,
        in_specs=[VMEM] * (1 + len(pieces)),
        out_specs=VMEM,
        out_shape=jax.ShapeDtypeStruct((rows, LANES), jnp.float32),
        compiler_params=params(16),
        cost_estimate=cost(*COST_NEAR[chunk]),
        name="near",
    )(fields, *pieces)


def away_kernel(split, fields, *rest):
    even, odd, first, outs = rest[:4], rest[4:8], rest[8], rest[9:]
    m = place() // 4
    half = LANES // 2
    rows = fields.shape[0]
    folded = outs[0].shape[-2]

    def emit(to, value):
        if not split:
            outs[0][to] = value.astype(outs[0].dtype)
            return
        hop = to ^ lax.axis_index("tile")
        for k, out in enumerate(outs):

            @pl.when(hop == k)
            def _(out=out):
                out[...] = value.astype(out.dtype)

    def body(pieces):
        low = lax.broadcasted_iota(jnp.int32, (folded, LANES), 1) < half
        for e, total in enumerate([first[...], products_of(fields, pieces)]):
            turned = pltpu.roll(total, half, 1)
            top, bottom = slice(0, folded), slice(rows - folded, rows)
            emit(2 * (m ^ e), jnp.where(low, total[top], turned[bottom]))
            emit(2 * (m ^ e) + 1, jnp.where(low, turned[top], total[bottom]))

    by_core(even, odd, body)


def away_scores(fields, pieces, near, split, chunk):
    folded = fold_rows(fields.shape[0])
    if split:
        out_shape = [jax.ShapeDtypeStruct((folded, LANES), jnp.float32)] + [
            jax.ShapeDtypeStruct((folded, LANES), jnp.bfloat16)
        ] * 3
    else:
        out_shape = [jax.ShapeDtypeStruct((4, folded, LANES), jnp.float32)]
    return pl.pallas_call(
        functools.partial(away_kernel, split),
        in_specs=[VMEM] * (2 + len(pieces)),
        out_specs=[VMEM] * len(out_shape),
        out_shape=out_shape,
        compiler_params=params(18),
        cost_estimate=cost(*COST_AWAY[chunk]),
        name="away",
    )(fields, *pieces, near)


def raw_kernel(fields, *rest):
    even, odd, out = rest[:4], rest[4:8], rest[8]

    def body(pieces):
        out[...] = products_of(fields, pieces)

    by_core(even, odd, body)


def raw_scores(fields, pieces, chunk):
    rows = fields.shape[0]
    return pl.pallas_call(
        raw_kernel,
        in_specs=[VMEM] * (1 + len(pieces)),
        out_specs=VMEM,
        out_shape=jax.ShapeDtypeStruct((rows, LANES), jnp.float32),
        compiler_params=params(16),
        cost_estimate=cost(*COST_AWAY[chunk]),
        name="raw",
    )(fields, *pieces)


def last_kernel(split, fields, *rest):
    even, odd, earlier, outs = rest[:4], rest[4:8], rest[8:11], rest[11:]
    m = place() // 4
    half = LANES // 2
    low = lax.broadcasted_iota(jnp.int32, earlier[0].shape, 1) < half

    def emit(to, value):
        if not split:
            outs[0][to] = value.astype(outs[0].dtype)
            return
        hop = to ^ lax.axis_index("tile")
        for k, out in enumerate(outs):

            @pl.when(hop == k)
            def _(out=out):
                out[...] = value.astype(out.dtype)

    def body(pieces):
        second = products_of(fields, pieces)
        pairs = [(earlier[0][...], earlier[2][...]), (earlier[1][...], second)]
        for e, (a, b) in enumerate(pairs):
            emit(2 * (m ^ e), jnp.where(low, a, pltpu.roll(b, half, 1)))
            emit(2 * (m ^ e) + 1, jnp.where(low, pltpu.roll(a, half, 1), b))

    by_core(even, odd, body)


def last_scores(fields, pieces, earlier, split):
    rows = fields.shape[0]
    if split:
        out_shape = [jax.ShapeDtypeStruct((rows, LANES), jnp.float32)] + [
            jax.ShapeDtypeStruct((rows, LANES), jnp.bfloat16)
        ] * 3
    else:
        out_shape = [jax.ShapeDtypeStruct((4, rows, LANES), jnp.float32)]
    return pl.pallas_call(
        functools.partial(last_kernel, split),
        in_specs=[VMEM] * (1 + len(pieces) + len(earlier)),
        out_specs=[VMEM] * len(out_shape),
        out_shape=out_shape,
        compiler_params=params(18),
        cost_estimate=cost(*COST_AWAY[1]),
        name="last",
    )(fields, *pieces, *earlier)


def fold_rows(rows):
    return -(-rows // 32) * 16


def final_kernel(*refs):
    parts, out = refs[:-1], refs[-1]
    rows, half = out.shape[0], LANES // 2
    folded = parts[0].shape[0]
    low = lax.broadcasted_iota(jnp.int32, (folded, LANES), 1) < half
    a, b = [
        parts[c][...] + sum(part[...].astype(jnp.float32) for part in parts[c + 1 : c + 4])
        for c in (0, 4)
    ]
    skip = 2 * folded - rows
    out[:folded, :] = jnp.where(low, a, pltpu.roll(b, half, 1))
    below = jnp.where(low, pltpu.roll(a, half, 1), b)
    out[folded:, :] = below[skip:]


def final(parts, rows):
    return pl.pallas_call(
        final_kernel,
        in_specs=[VMEM] * len(parts),
        out_specs=VMEM,
        out_shape=jax.ShapeDtypeStruct((rows, LANES), jnp.float32),
        compiler_params=params(8),
        name="final",
    )(*parts)


def over_tile(x, flip):
    return lax.ppermute(x, "tile", [(i, i ^ flip) for i in range(4)])


def plane_permute(x, to):
    pairs = []
    for m in range(2):
        for a in range(2):
            for c in range(2):
                tm, ta, tc = to(m, a, c)
                pairs.append((m * 4 + a * 2 + c, tm * 4 + ta * 2 + tc))
    return lax.ppermute(x, PLANE, pairs)


def over_core(x):
    return plane_permute(x, lambda m, a, c: (m, a, 1 - c))


def over_first(x):
    return plane_permute(x, lambda m, a, c: (m, 1 - a, c) if c == 0 else (1 - m, a, c))


def over_second(x):
    return plane_permute(x, lambda m, a, c: (1 - m, a, c) if c == 0 else (m, 1 - a, c))


def gather_plane(piece, after):
    def tie(x, name):
        return lax.optimization_barrier((x, *after[name]))[0] if after.get(name) else x

    r1 = over_first(piece)
    other = over_core(tie(piece, "other") if DIRECT else piece)
    if DIRECT:
        r2 = over_second(tie(piece, "r2"))
    else:
        r2 = over_first(tie(other, "r2"))
    d = over_second(tie(r1, "d"))
    s1, s2, s3 = over_core(tie(r1, "s1")), over_core(tie(r2, "s2")), over_core(tie(d, "s3"))
    if DIRECT:
        return (piece, other, r1, s2, s1, r2), (r2, s1, d, s3, s2, r1, s3, d), r1, r2, d
    return (piece, other, r1, r2, s1, s2), (s2, s1, d, s3, r2, r1, s3, d), r1, r2, d


def tile_table(tile_source, tile_band, tile_block, blocks, bands, z):
    tiles = tile_source.shape[0]
    owner = tile_band[:, 0]
    if bands == 4:
        hop = owner ^ z
        is_late = hop == 2
        slot = jnp.where(hop == 3, 2, jnp.where(is_late, 0, hop))
    else:
        is_late = jnp.zeros_like(owner, dtype=bool)
        slot = owner
    count = blocks // GROUPS
    side = tile_block // count
    row = slot * count + tile_block - side * count
    order = jnp.arange(tiles, dtype=jnp.int32)
    code = (order << 19) | (row << 9) | (side << 6) | tile_source
    key = order + jnp.where(is_late, tiles, 0)
    rank = jnp.sum((key[None, :] < key[:, None]).astype(jnp.int32), 1)
    size = tiles + 2 * UNROLL
    place_of = jnp.arange(size, dtype=jnp.int32)
    listed = jnp.sum(jnp.where(rank[None, :] == place_of[:, None], code[None, :], 0), 1)
    soon = jnp.sum(jnp.where(is_late, 0, 1))
    return jnp.where(place_of == size - 1, soon, listed).astype(jnp.int32)


def on_device(fields, remap_tiles, tile_source, tile_band, tile_block, patterns):
    bands = lax.axis_size("tile")
    day_count, var_count, source_cells = fields.shape
    row_count = day_count * var_count
    source_blocks = source_cells // LANES
    pattern_count = patterns.shape[1]
    z = lax.axis_index("tile")
    rows = fields.transpose(1, 0, 2).reshape(row_count, source_cells)
    table = tile_table(
        tile_source, tile_band, tile_block, patterns.shape[0] // LANES, bands, z
    )
    owns, totals, lasts, pieces = [], [], [], []
    for chunk in range(CHUNKS):
        own = pack(patterns, chunk, owns[-1:])
        owns.append(own)
        if bands == 4:
            if chunk and TIE_OWN:
                own = lax.optimization_barrier((own, far))[0]
            far = over_tile(own, 3)
            near = over_tile(own, 1)
            known = [own, near, far]
            if chunk and TIE_HOP:
                pieces.append(late(table, remap_tiles, totals[0], lasts[0]))
                passed = lax.optimization_barrier((far, pieces[0]))[0]
            else:
                passed = far
            lasts.append(over_tile(passed, 1))
        else:
            gathered = lax.all_gather(own, "tile", axis=0)
            known = [gathered.reshape((-1,) + gathered.shape[2:])]
            lasts.append(own)
        totals.append(early(table, remap_tiles, known, source_blocks))
    if TIE_EARLY:
        totals = list(lax.optimization_barrier(totals))
    sums, past, raw = [], {}, []
    for chunk in range(CHUNKS):

        def after(x, names):
            held = [past[name] for name in names if name in past]
            return lax.optimization_barrier((x, *held))[0] if held else x

        if chunk < len(pieces):
            piece = pieces[chunk]
        else:
            total = after(totals[chunk], TIE_LATE)
            piece = late(table, remap_tiles, total, lasts[chunk])
        near, away, r1, r2, d = gather_plane(piece, {k: [past[n] for n in v if n in past] for k, v in TIE_SWAP.items()})
        part = near_scores(rows, [after(near[0], TIE_NEAR), *near[1:]], chunk)
        raw.append(part)
        if MERGED and chunk == 0:
            far_part = raw_scores(rows, away, chunk)
            raw.append(far_part)
            past = dict(piece=piece, other=near[1], r1=r1, r2=r2, d=d, near=part, away=far_part)
            continue
        if MERGED:
            parts = list(last_scores(rows, away, raw, bands == 4))
        else:
            parts = list(away_scores(rows, away, part, bands == 4, chunk))
        past = dict(piece=piece, other=near[1], r1=r1, r2=r2, d=d, near=part, away=parts[0])
        if bands == 4:
            for k in (1, 2, 3):
                parts[k] = over_tile(parts[k], k)
            sums += parts
            past["sum1"], past["sum2"], past["sum3"] = parts[1:]
        elif MERGED:
            sums.append(parts[0])
        else:
            folded = parts[0]
            half, skip = LANES // 2, 2 * folded.shape[1] - row_count
            sums.append(
                jnp.concatenate([folded[:, :, :half], folded[:, skip:, half:]], 1)
            )
    if bands == 4:
        if MERGED:
            result = sums[0]
            for moved in sums[1:]:
                result = result + moved.astype(jnp.float32)
        else:
            result = final(sums, row_count)
    else:
        partial = jnp.concatenate(sums, 2).transpose(1, 0, 2).reshape(row_count, pattern_count)
        result = lax.psum_scatter(partial, "tile", scatter_dimension=1, tiled=True)
    return result.reshape(var_count, day_count, pattern_count // bands).transpose(1, 0, 2)


def solution(mesh):
    return jax.shard_map(
        on_device,
        mesh=mesh,
        in_specs=(
            P(("member", "day"), None, "tile"),
            P("tile", None, None),
            P("tile"),
            P("tile", None),
            P("tile"),
            P("tile", None),
        ),
        out_specs=P(("member", "day"), None, "tile"),
        check_vma=False,
    )
```

```python
import functools

import jax
import jax.numpy as jnp
from jax import lax
from jax.experimental import pallas as pl
from jax.experimental.pallas import tpu as pltpu
from jax.sharding import PartitionSpec as P

PLANE = ("member", "day")
LANES = 128
CHUNKS = 2
GROUPS = 2 * CHUNKS
WIDTH = LANES // GROUPS
UNROLL = 32
EARLY = 32
LATE = 16
COST_EARLY = (11, 0.4)
COST_LATE = (8, 0.2)
COST_NEAR = [(5, 0.6), (5, 0.6)]
COST_AWAY = [(5, 0.6), (5, 0.6)]
DIRECT = True
MERGED = True
TIE_LATE = []
TIE_OWN = True
TIE_HOP = True
TIE_EARLY = False
TIE_SWAP = {'s1': ['near'], 's2': ['near']}
TIE_NEAR = []
PARTS = 1
MIB = 2**20

VMEM = pl.BlockSpec(memory_space=pltpu.VMEM)
SMEM = pl.BlockSpec(memory_space=pltpu.SMEM)
ANY = pl.BlockSpec(memory_space=pl.ANY)


def place():
    return lax.axis_index("member") * 4 + lax.axis_index("day")


def params(mib):
    return pltpu.CompilerParams(vmem_limit_bytes=mib * MIB)


def cost(mib, gflop):
    return pl.CostEstimate(
        flops=int(gflop * 1e9), bytes_accessed=int(mib * MIB), transcendentals=0
    )


def group_of(shape):
    return lax.broadcasted_iota(jnp.int32, shape, 1) // WIDTH


def pick(mask_of, values):
    out = values[-1]
    for k in range(len(values) - 2, -1, -1):
        out = jnp.where(mask_of(k), values[k], out)
    return out


def pack_kernel(parts, chunk, patterns, *rest):
    out, held, sems = rest[-3:]
    p = place()
    chip, core = p // 2, lax.rem(p, 2)
    count = out.shape[0]
    step = count // parts
    columns = pl.ds(pl.multiple_of(chip * LANES, LANES), LANES)
    copies = []
    for part in range(parts):
        for group in range(GROUPS):
            rows = pl.ds((group * count + part * step) * LANES, step * LANES)
            copies.append(
                pltpu.make_async_copy(
                    patterns.at[rows, columns], held.at[rows, :], sems.at[part, group]
                )
            )
            copies[-1].start()
    shape = (GROUPS * LANES, LANES)
    k = lax.broadcasted_iota(jnp.int32, shape, 0)
    n = lax.broadcasted_iota(jnp.int32, shape, 1)
    wanted = chunk * (LANES // CHUNKS) + core * WIDTH + n % WIDTH
    chosen = (k // LANES == n // WIDTH) & (k % LANES == wanted)
    choose = jnp.where(chosen, 1.0, 0.0).astype(held.dtype)
    for part in range(parts):
        for group in range(GROUPS):
            copies[part * GROUPS + group].wait()
        blocks = [
            held[pl.ds((group * count + part * step) * LANES, step * LANES), :]
            for group in range(GROUPS)
        ]
        both = jnp.dot(jnp.concatenate(blocks, 1), choose, preferred_element_type=jnp.float32)
        out[part * step : (part + 1) * step] = both.astype(out.dtype).reshape(step, LANES, LANES)


def pack(patterns, chunk, after):
    rows = patterns.shape[0]
    count = rows // LANES // GROUPS
    parts = PARTS
    return pl.pallas_call(
        functools.partial(pack_kernel, parts, chunk),
        in_specs=[ANY] * (1 + len(after)),
        out_specs=VMEM,
        out_shape=jax.ShapeDtypeStruct((count, LANES, LANES), patterns.dtype),
        scratch_shapes=[
            pltpu.VMEM((rows, LANES), patterns.dtype),
            pltpu.SemaphoreType.DMA((parts, GROUPS)),
        ],
        compiler_params=params(58),
        cost_estimate=cost(2.3, 0.15),
        name="pack",
    )(patterns, *after)


def add_tiles(unroll, table, start, end, weights, held, total):
    group = group_of((LANES, LANES))

    @pl.loop(0, (end - start + unroll - 1) // unroll)
    def _(step):
        products, targets = [], []
        for u in range(unroll):
            i = start + step * unroll + u
            code = table[i]
            side = jnp.where(i < end, (code >> 6) & 7, 7)
            targets.append(code & 63)
            rhs = held[(code >> 9) & 1023]
            rhs = jnp.where(group == side, rhs, jnp.zeros_like(rhs))
            products.append(
                jnp.dot(weights[code >> 19], rhs, preferred_element_type=jnp.float32)
            )
        for target, product in zip(targets, products):
            total[target] += product


def early_kernel(table, weights, *rest):
    bands, total, held, sems = rest[:-3], rest[-3], rest[-2], rest[-1]
    count = bands[0].shape[0]
    copies = [
        pltpu.make_async_copy(band, held.at[pl.ds(i * count, count)], sems.at[i])
        for i, band in enumerate(bands)
    ]
    for copy in copies:
        copy.start()
    total[...] = jnp.zeros_like(total)
    for copy in copies:
        copy.wait()
    add_tiles(EARLY, table, 0, table[table.shape[0] - 1], weights, held, total)


def early(table, weights, bands, source_blocks):
    count = bands[0].shape[0]
    return pl.pallas_call(
        early_kernel,
        in_specs=[SMEM, VMEM] + [ANY] * len(bands),
        out_specs=VMEM,
        out_shape=jax.ShapeDtypeStruct((source_blocks, LANES, LANES), jnp.float32),
        scratch_shapes=[
            pltpu.VMEM((count * len(bands), LANES, LANES), weights.dtype),
            pltpu.SemaphoreType.DMA((len(bands),)),
        ],
        compiler_params=params(10 + count * len(bands) * LANES * LANES * 2 // MIB),
        cost_estimate=cost(*COST_EARLY),
        name="early",
    )(table, weights, *bands)


def late_kernel(table, weights, given, band, packed, total):
    total[...] = jnp.zeros_like(total)
    start = table[table.shape[0] - 1]
    add_tiles(LATE, table, start, weights.shape[0], weights, band, total)
    blocks = packed.shape[0]
    me = lax.rem(place(), GROUPS)
    group = group_of((LANES, LANES))
    for j in range(blocks):
        places = [h * blocks + j for h in range(GROUPS)]
        sums = [given[i] + total[i] for i in places]
        out = None
        for r in range(GROUPS):
            want = lax.rem(group + (r + GROUPS) - me, GROUPS)
            term = pick(lambda k: want == k, sums)
            if r:
                term = pltpu.roll(term, r * WIDTH, 1)
            out = term if out is None else out + term
        packed[j] = out.astype(packed.dtype)


def late(table, weights, total, band):
    source_blocks = total.shape[0]
    return pl.pallas_call(
        late_kernel,
        in_specs=[SMEM, VMEM, VMEM, VMEM],
        out_specs=VMEM,
        out_shape=jax.ShapeDtypeStruct((source_blocks // GROUPS, LANES, LANES), weights.dtype),
        scratch_shapes=[
            pltpu.VMEM(total.shape, jnp.float32),
        ],
        compiler_params=params(14),
        cost_estimate=cost(*COST_LATE),
        name="late",
    )(table, weights, total, band)


def products_of(fields, pieces):
    depth = fields.shape[1] // GROUPS
    across = lax.rem(place(), 4) // 2
    group = group_of((depth, LANES))
    values = [piece[...].reshape(depth, LANES) for piece in pieces]
    near, away = 2 * across, 2 * (1 - across)
    members = [near, near + 1, away, away + 1]
    total = None
    for h in range(GROUPS):
        index = [lax.rem(i + h, GROUPS) for i in members]
        term = jnp.dot(
            fields[:, h * depth : (h + 1) * depth],
            pick(lambda k: group == index[k], values),
            preferred_element_type=jnp.float32,
        )
        if h:
            term = pltpu.roll(term, LANES - h * WIDTH, 1)
        total = term if total is None else total + term
    return total


def by_core(even, odd, body):
    core = lax.rem(place(), 2)

    @pl.when(core == 0)
    def _():
        body(even)

    @pl.when(core == 1)
    def _():
        body(odd)


def near_kernel(fields, mine, other, *rest):
    x_even, x_odd, out = rest[:2], rest[2:4], rest[4]

    def body(pieces):
        out[...] = products_of(fields, pieces)

    by_core([mine, other, *x_even], [other, mine, *x_odd], body)


def near_scores(fields, pieces, chunk):
    rows = fields.shape[0]
    return pl.pallas_call(
        near_kernel,
        in_specs=[VMEM] * (1 + len(pieces)),
        out_specs=VMEM,
        out_shape=jax.ShapeDtypeStruct((rows, LANES), jnp.float32),
        compiler_params=params(16),
        cost_estimate=cost(*COST_NEAR[chunk]),
        name="near",
    )(fields, *pieces)


def away_kernel(split, fields, *rest):
    even, odd, first, outs = rest[:4], rest[4:8], rest[8], rest[9:]
    m = place() // 4
    half = LANES // 2
    rows = fields.shape[0]
    folded = outs[0].shape[-2]

    def emit(to, value):
        if not split:
            outs[0][to] = value.astype(outs[0].dtype)
            return
        hop = to ^ lax.axis_index("tile")
        for k, out in enumerate(outs):

            @pl.when(hop == k)
            def _(out=out):
                out[...] = value.astype(out.dtype)

    def body(pieces):
        low = lax.broadcasted_iota(jnp.int32, (folded, LANES), 1) < half
        for e, total in enumerate([first[...], products_of(fields, pieces)]):
            turned = pltpu.roll(total, half, 1)
            top, bottom = slice(0, folded), slice(rows - folded, rows)
            emit(2 * (m ^ e), jnp.where(low, total[top], turned[bottom]))
            emit(2 * (m ^ e) + 1, jnp.where(low, turned[top], total[bottom]))

    by_core(even, odd, body)


def away_scores(fields, pieces, near, split, chunk):
    folded = fold_rows(fields.shape[0])
    if split:
        out_shape = [jax.ShapeDtypeStruct((folded, LANES), jnp.float32)] + [
            jax.ShapeDtypeStruct((folded, LANES), jnp.bfloat16)
        ] * 3
    else:
        out_shape = [jax.ShapeDtypeStruct((4, folded, LANES), jnp.float32)]
    return pl.pallas_call(
        functools.partial(away_kernel, split),
        in_specs=[VMEM] * (2 + len(pieces)),
        out_specs=[VMEM] * len(out_shape),
        out_shape=out_shape,
        compiler_params=params(18),
        cost_estimate=cost(*COST_AWAY[chunk]),
        name="away",
    )(fields, *pieces, near)


def raw_kernel(fields, *rest):
    even, odd, out = rest[:4], rest[4:8], rest[8]

    def body(pieces):
        out[...] = products_of(fields, pieces)

    by_core(even, odd, body)


def raw_scores(fields, pieces, chunk):
    rows = fields.shape[0]
    return pl.pallas_call(
        raw_kernel,
        in_specs=[VMEM] * (1 + len(pieces)),
        out_specs=VMEM,
        out_shape=jax.ShapeDtypeStruct((rows, LANES), jnp.float32),
        compiler_params=params(16),
        cost_estimate=cost(*COST_AWAY[chunk]),
        name="raw",
    )(fields, *pieces)


def both_kernel(fields, *rest):
    away, near, outs = rest[:8], rest[8:14], rest[14:]
    raw_kernel(fields, *away, outs[0])
    near_kernel(fields, *near, outs[1])


def both_scores(fields, away, near):
    rows = fields.shape[0]
    return pl.pallas_call(
        both_kernel,
        in_specs=[VMEM] * (1 + len(away) + len(near)),
        out_specs=[VMEM] * 2,
        out_shape=[jax.ShapeDtypeStruct((rows, LANES), jnp.float32)] * 2,
        compiler_params=params(20),
        cost_estimate=cost(*COST_AWAY[1]),
        name="both",
    )(fields, *away, *near)


def last_kernel(split, fields, *rest):
    even, odd, earlier, outs = rest[:4], rest[4:8], rest[8:11], rest[11:]
    m = place() // 4
    half = LANES // 2
    low = lax.broadcasted_iota(jnp.int32, earlier[0].shape, 1) < half

    def emit(to, value):
        if not split:
            outs[0][to] = value.astype(outs[0].dtype)
            return
        hop = to ^ lax.axis_index("tile")
        for k, out in enumerate(outs):

            @pl.when(hop == k)
            def _(out=out):
                out[...] = value.astype(out.dtype)

    def body(pieces):
        second = products_of(fields, pieces)
        pairs = [(earlier[0][...], earlier[2][...]), (earlier[1][...], second)]
        for e, (a, b) in enumerate(pairs):
            emit(2 * (m ^ e), jnp.where(low, a, pltpu.roll(b, half, 1)))
            emit(2 * (m ^ e) + 1, jnp.where(low, pltpu.roll(a, half, 1), b))

    by_core(even, odd, body)


def last_scores(fields, pieces, earlier, split):
    rows = fields.shape[0]
    if split:
        out_shape = [jax.ShapeDtypeStruct((rows, LANES), jnp.float32)] + [
            jax.ShapeDtypeStruct((rows, LANES), jnp.bfloat16)
        ] * 3
    else:
        out_shape = [jax.ShapeDtypeStruct((4, rows, LANES), jnp.float32)]
    return pl.pallas_call(
        functools.partial(last_kernel, split),
        in_specs=[VMEM] * (1 + len(pieces) + len(earlier)),
        out_specs=[VMEM] * len(out_shape),
        out_shape=out_shape,
        compiler_params=params(18),
        cost_estimate=cost(*COST_AWAY[1]),
        name="last",
    )(fields, *pieces, *earlier)


def fold_rows(rows):
    return -(-rows // 32) * 16


def final_kernel(*refs):
    parts, out = refs[:-1], refs[-1]
    rows, half = out.shape[0], LANES // 2
    folded = parts[0].shape[0]
    low = lax.broadcasted_iota(jnp.int32, (folded, LANES), 1) < half
    a, b = [
        parts[c][...] + sum(part[...].astype(jnp.float32) for part in parts[c + 1 : c + 4])
        for c in (0, 4)
    ]
    skip = 2 * folded - rows
    out[:folded, :] = jnp.where(low, a, pltpu.roll(b, half, 1))
    below = jnp.where(low, pltpu.roll(a, half, 1), b)
    out[folded:, :] = below[skip:]


def final(parts, rows):
    return pl.pallas_call(
        final_kernel,
        in_specs=[VMEM] * len(parts),
        out_specs=VMEM,
        out_shape=jax.ShapeDtypeStruct((rows, LANES), jnp.float32),
        compiler_params=params(8),
        name="final",
    )(*parts)


def over_tile(x, flip):
    return lax.ppermute(x, "tile", [(i, i ^ flip) for i in range(4)])


def plane_permute(x, to):
    pairs = []
    for m in range(2):
        for a in range(2):
            for c in range(2):
                tm, ta, tc = to(m, a, c)
                pairs.append((m * 4 + a * 2 + c, tm * 4 + ta * 2 + tc))
    return lax.ppermute(x, PLANE, pairs)


def over_core(x):
    return plane_permute(x, lambda m, a, c: (m, a, 1 - c))


def over_first(x):
    return plane_permute(x, lambda m, a, c: (m, 1 - a, c) if c == 0 else (1 - m, a, c))


def over_second(x):
    return plane_permute(x, lambda m, a, c: (1 - m, a, c) if c == 0 else (m, 1 - a, c))


def gather_plane(piece, after):
    def tie(x, name):
        return lax.optimization_barrier((x, *after[name]))[0] if after.get(name) else x

    r1 = over_first(piece)
    other = over_core(tie(piece, "other") if DIRECT else piece)
    if DIRECT:
        r2 = over_second(tie(piece, "r2"))
    else:
        r2 = over_first(tie(other, "r2"))
    d = over_second(tie(r1, "d"))
    s1, s2, s3 = over_core(tie(r1, "s1")), over_core(tie(r2, "s2")), over_core(tie(d, "s3"))
    if DIRECT:
        return (piece, other, r1, s2, s1, r2), (r2, s1, d, s3, s2, r1, s3, d), r1, r2, d
    return (piece, other, r1, r2, s1, s2), (s2, s1, d, s3, r2, r1, s3, d), r1, r2, d


def tile_table(tile_source, tile_band, tile_block, blocks, bands, z):
    tiles = tile_source.shape[0]
    owner = tile_band[:, 0]
    if bands == 4:
        hop = owner ^ z
        is_late = hop == 2
        slot = jnp.where(hop == 3, 2, jnp.where(is_late, 0, hop))
    else:
        is_late = jnp.zeros_like(owner, dtype=bool)
        slot = owner
    count = blocks // GROUPS
    side = tile_block // count
    row = slot * count + tile_block - side * count
    order = jnp.arange(tiles, dtype=jnp.int32)
    code = (order << 19) | (row << 9) | (side << 6) | tile_source
    key = order + jnp.where(is_late, tiles, 0)
    rank = jnp.sum((key[None, :] < key[:, None]).astype(jnp.int32), 1)
    size = tiles + 2 * UNROLL
    place_of = jnp.arange(size, dtype=jnp.int32)
    listed = jnp.sum(jnp.where(rank[None, :] == place_of[:, None], code[None, :], 0), 1)
    soon = jnp.sum(jnp.where(is_late, 0, 1))
    return jnp.where(place_of == size - 1, soon, listed).astype(jnp.int32)


def on_device(fields, remap_tiles, tile_source, tile_band, tile_block, patterns):
    bands = lax.axis_size("tile")
    day_count, var_count, source_cells = fields.shape
    row_count = day_count * var_count
    source_blocks = source_cells // LANES
    pattern_count = patterns.shape[1]
    z = lax.axis_index("tile")
    rows = fields.transpose(1, 0, 2).reshape(row_count, source_cells)
    table = tile_table(
        tile_source, tile_band, tile_block, patterns.shape[0] // LANES, bands, z
    )
    owns, totals, lasts, pieces = [], [], [], []
    for chunk in range(CHUNKS):
        own = pack(patterns, chunk, owns[-1:])
        owns.append(own)
        if bands == 4:
            if chunk and TIE_OWN:
                own = lax.optimization_barrier((own, far))[0]
            far = over_tile(own, 3)
            near = over_tile(own, 1)
            known = [own, near, far]
            if chunk and TIE_HOP:
                pieces.append(late(table, remap_tiles, totals[0], lasts[0]))
                passed = lax.optimization_barrier((far, pieces[0]))[0]
            else:
                passed = far
            lasts.append(over_tile(passed, 1))
        else:
            gathered = lax.all_gather(own, "tile", axis=0)
            known = [gathered.reshape((-1,) + gathered.shape[2:])]
            lasts.append(own)
        totals.append(early(table, remap_tiles, known, source_blocks))
    if TIE_EARLY:
        totals = list(lax.optimization_barrier(totals))
    sums, past, raw = [], {}, []
    for chunk in range(CHUNKS):

        def after(x, names):
            held = [past[name] for name in names if name in past]
            return lax.optimization_barrier((x, *held))[0] if held else x

        if chunk < len(pieces):
            piece = pieces[chunk]
        else:
            total = after(totals[chunk], TIE_LATE)
            piece = late(table, remap_tiles, total, lasts[chunk])
        near, away, r1, r2, d = gather_plane(piece, {k: [past[n] for n in v if n in past] for k, v in TIE_SWAP.items()})
        if chunk == 0:
            part = near_scores(rows, near, chunk)
            raw.append(part)
            kept = away
            past = dict(piece=piece, other=near[1], r1=r1, r2=r2, d=d, near=part)
            continue
        far_part, part = both_scores(rows, kept, near)
        raw += [far_part, part]
        if MERGED:
            parts = list(last_scores(rows, away, raw, bands == 4))
        else:
            parts = list(away_scores(rows, away, part, bands == 4, chunk))
        past = dict(piece=piece, other=near[1], r1=r1, r2=r2, d=d, near=part, away=parts[0])
        if bands == 4:
            for k in (1, 2, 3):
                parts[k] = over_tile(parts[k], k)
            sums += parts
            past["sum1"], past["sum2"], past["sum3"] = parts[1:]
        elif MERGED:
            sums.append(parts[0])
        else:
            folded = parts[0]
            half, skip = LANES // 2, 2 * folded.shape[1] - row_count
            sums.append(
                jnp.concatenate([folded[:, :, :half], folded[:, skip:, half:]], 1)
            )
    if bands == 4:
        if MERGED:
            result = sums[0]
            for moved in sums[1:]:
                result = result + moved.astype(jnp.float32)
        else:
            result = final(sums, row_count)
    else:
        partial = jnp.concatenate(sums, 2).transpose(1, 0, 2).reshape(row_count, pattern_count)
        result = lax.psum_scatter(partial, "tile", scatter_dimension=1, tiled=True)
    return result.reshape(var_count, day_count, pattern_count // bands).transpose(1, 0, 2)


def solution(mesh):
    return jax.shard_map(
        on_device,
        mesh=mesh,
        in_specs=(
            P(("member", "day"), None, "tile"),
            P("tile", None, None),
            P("tile"),
            P("tile", None),
            P("tile"),
            P("tile", None),
        ),
        out_specs=P(("member", "day"), None, "tile"),
        check_vma=False,
    )
```
